256 devices in a mesh: dp: 4 (over z_lo), member: 2 (over z_hi), space: 32 (over x, y, core).
Axes of the slice: x: 4, y: 4, z: 8 (z_hi: 2, z_lo: 4; z = z_hi * 4 + z_lo), core: 2. Of those that a mesh axis runs over, the one named last changes fastest.
Arguments:
- grid_in: bfloat16 [4, 84, 16384], P('dp', None, 'space'), may hold values from -6 to 6
- target: bfloat16 [4, 84, 16384], P('dp', None, 'space'), may hold values from -6 to 6
- noise: float32 [4, 8, 32], P('dp', 'member'), may hold values from -6 to 6
- neighbours: int32 [64, 3], P('space'), may hold values from 0 to 63, as said below
- enc_index: int32 [4096, 4], P('space'), may hold values from 0 to 16383, as said below
- dec_index: int32 [16384, 3], P('space'), may hold values from 0 to 4095, as said below
- w_in: bfloat16 [84, 768], replicated, may hold values from -0.625 to 0.625
- w_gamma: float32 [32, 768], replicated, may hold values from -0.6 to 0.6
- w_beta: float32 [32, 768], replicated, may hold values from -0.6 to 0.6
- w_qkv: bfloat16 [768, 2304], replicated, may hold values from -60 to 60
- w_o: bfloat16 [768, 768], replicated, may hold values from -0.8984375 to 0.8984375
- readout_matrix: bfloat16 [84, 768], replicated, may hold values from -0.21875 to 0.21875
Outputs:
- predicted_states: bfloat16 [4, 8, 84, 16384], P('dp', 'member', None, 'space')
- objective_mean: float32 [], replicated
- unit_descent_slope: float32 [84, 768], replicated
The draws below stay inside these ranges and needn't reach their ends.
Inputs may be any that keep to these rules, and one draw needn't show every extreme that they name: `neighbours`: row w lists three different windows other than w whose ids differ from w by 1 or 2, counted around the 64 windows. `enc_index`: rows j * 128 to (j + 1) * 128 - 1 name only grid points j * 512 to (j + 1) * 512 - 1. `dec_index`: rows j * 512 to (j + 1) * 512 - 1 name only tokens j * 128 to (j + 1) * 128 - 1.
All inputs are finite; a program needn't handle non-finite values.
Results may differ from the reference program's by a relative error of at most 0.0065.
The reference program's roundings to bfloat16 on the way count: a program that leaves them out, or rounds other values in their place, can miss the bound.
Values may be sent and summed in bfloat16 or wider, within the bound.
No kernel may reach another device: no remote copies, remote signals or barrier semaphores. Data moves between devices by JAX's collectives and lax.ppermute only.
A program may use at most 128 MiB of HBM per device.

```python
import jax
import jax.numpy as jnp
from jax import lax

V = 84
D = 768
HEADS = 12
HD = 64
NZ = 32
WIN = 64
NBR = 3
K_ENC = 4
K_DEC = 3
TOK_DEV = 128
G_DEV = 512
SAMPLES = 4
MEMBERS = 8
TOKENS = 4096
GRID = 16384
N_SPACE = 32


def draw_neighbours(key, part):
    total = TOK_DEV // WIN * N_SPACE
    shifts = jnp.array([-2, -1, 1, 2], dtype=jnp.int32)
    dropped = jax.random.randint(jax.random.fold_in(key, 11), (total, 1), 0, 4)
    slots = jnp.arange(3, dtype=jnp.int32)[None, :]
    picked = slots + (slots >= dropped).astype(jnp.int32)
    return ((jnp.arange(total, dtype=jnp.int32)[:, None] + shifts[picked]) % total).astype(jnp.int32)


def draw_enc_index(key, part):
    rows = TOK_DEV * N_SPACE
    blocks = jnp.arange(rows, dtype=jnp.int32) // TOK_DEV
    offsets = jax.random.randint(jax.random.fold_in(key, 23), (rows, K_ENC), 0, G_DEV)
    return (blocks[:, None] * G_DEV + offsets).astype(jnp.int32)


def draw_dec_index(key, part):
    rows = G_DEV * N_SPACE
    blocks = jnp.arange(rows, dtype=jnp.int32) // G_DEV
    offsets = jax.random.randint(jax.random.fold_in(key, 37), (rows, K_DEC), 0, TOK_DEV)
    return (blocks[:, None] * TOK_DEV + offsets).astype(jnp.int32)


def draw_w_qkv(key, part):
    base = jax.random.normal(jax.random.fold_in(key, 41), (D, 3 * D), jnp.float32)
    base = jnp.clip(base, -6.0, 6.0) / jnp.sqrt(jnp.float32(D))
    return base.astype(jnp.bfloat16)


def shard_levels(own_key, extent, cuts, smallest, high):
    def one(dim, parts):
        draws = jax.random.uniform(jax.random.fold_in(jax.random.fold_in(own_key, 6), dim), (parts,), jnp.float32, smallest / len(cuts), high / len(cuts))
        return jnp.repeat(jnp.exp(draws), extent[dim] // parts).reshape((-1,) + (1,) * (len(extent) - dim - 1))

    gain = one(*cuts[0])
    for cut in cuts[1:]:
        gain = gain * one(*cut)
    return gain


def normal_values(stream_key, shape, deviation, limit, split=(), held_as=jnp.bfloat16):
    values = jax.random.normal(stream_key, shape, jnp.float32) * deviation
    if len(split) > 0:
        values = shard_levels(stream_key, shape, split, -0.22, 0.18) * values
    return jnp.clip(values, min=-limit, max=limit).astype(held_as)


def setup_inputs(seed: int = 0) -> dict:
    arg_keys = jax.random.split(jax.random.key(seed), 13)
    return {
        "grid_in": normal_values(arg_keys[0], (SAMPLES, V, GRID), 1.0, 6.0, ((0, 4), (2, 32))),
        "target": normal_values(arg_keys[1], (SAMPLES, V, GRID), 1.0, 6.0, ((0, 4), (2, 32))),
        "noise": normal_values(arg_keys[2], (SAMPLES, MEMBERS, NZ), 1.0, 6.0, ((0, 4), (1, 2)), jnp.float32),
        "neighbours": draw_neighbours(jax.random.fold_in(arg_keys[12], 71), 0),
        "enc_index": draw_enc_index(jax.random.fold_in(arg_keys[12], 71), 0),
        "dec_index": draw_dec_index(jax.random.fold_in(arg_keys[12], 71), 0),
        "w_in": normal_values(arg_keys[6], (V, D), V ** -0.5, 0.625),
        "w_gamma": normal_values(arg_keys[7], (NZ, D), 0.1, 0.6, (), jnp.float32),
        "w_beta": normal_values(arg_keys[8], (NZ, D), 0.1, 0.6, (), jnp.float32),
        "w_qkv": draw_w_qkv(jax.random.fold_in(arg_keys[12], 71), 0),
        "w_o": normal_values(arg_keys[10], (D, D), 0.15, 0.8984375),
        "readout_matrix": normal_values(arg_keys[11], (V, D), D ** -0.5, 0.21875),
    }


EPSILON = 1e-06

def layer_norm(values):
    centre = values - lax.optimization_barrier(jnp.mean(values, axis=-1, keepdims=True))
    spread = lax.optimization_barrier(jnp.mean(centre * centre, axis=-1, keepdims=True))
    return centre / jnp.sqrt(spread + EPSILON)

def conditioning(noise_rows, w_gamma, w_beta):
    scaling_factors = 1.0 + jnp.dot(noise_rows, w_gamma, precision=lax.Precision.HIGHEST)
    shift_terms_list = jnp.dot(noise_rows, w_beta, precision=lax.Precision.HIGHEST)
    return (scaling_factors, shift_terms_list)

def reference(grid_in, target, noise, neighbours, enc_index, dec_index, w_in, w_gamma, w_beta, w_qkv, w_o, readout_matrix):
    windows = TOKENS // WIN
    window_order = jnp.concatenate([jnp.arange(windows, dtype=jnp.int32)[:, None], neighbours.astype(jnp.int32)], axis=1)
    score_scale = HD ** (-0.5)
    pair_mask = 1.0 - jnp.eye(MEMBERS, dtype=jnp.float32)
    score_sum = jnp.zeros((), jnp.float32)
    gradient = jnp.zeros((V, D), jnp.float32)
    prediction_results = []
    for sample in range(SAMPLES):
        predicted_quantities = grid_in[sample]
        embedded = jnp.dot(predicted_quantities.T, w_in, preferred_element_type=jnp.float32)
        states = embedded[enc_index[:, 0]]
        for column in range(1, K_ENC):
            states = states + embedded[enc_index[:, column]]
        states = states / K_ENC
        normed = layer_norm(states)
        scaling_factors, shift_terms_list = conditioning(noise[sample], w_gamma, w_beta)

        def realization_sweep(conditions):
            gain_one, bias_one = conditions
            inputs = (normed * gain_one + bias_one).astype(jnp.bfloat16)
            project = jnp.dot(inputs, w_qkv, preferred_element_type=jnp.float32).astype(jnp.bfloat16)
            queries = project[:, :D].reshape(windows, WIN, HEADS, HD).astype(jnp.float32)
            key_rows = project[:, D:2 * D].reshape(windows, WIN, HEADS, HD)[window_order]
            key_rows = key_rows.reshape(windows, (1 + NBR) * WIN, HEADS, HD).astype(jnp.float32)
            value_rows = project[:, 2 * D:].reshape(windows, WIN, HEADS, HD)[window_order]
            value_rows = value_rows.reshape(windows, (1 + NBR) * WIN, HEADS, HD).astype(jnp.float32)
            scores = jnp.einsum('wqhd,wkhd->whqk', queries, key_rows) * score_scale
            weights = lax.optimization_barrier(jax.nn.softmax(scores, axis=-1).astype(jnp.bfloat16))
            attended = jnp.einsum('whqk,wkhd->wqhd', weights.astype(jnp.float32), value_rows)
            attended = attended.astype(jnp.bfloat16).reshape(TOKENS, D)
            updated = states + jnp.dot(attended, w_o, preferred_element_type=jnp.float32)
            gathered = updated[dec_index[:, 0]]
            for column in range(1, K_DEC):
                gathered = gathered + updated[dec_index[:, column]]
            hidden_activations = (gathered / K_DEC).astype(jnp.bfloat16)
            predicted_states = (predicted_quantities.astype(jnp.float32) + jnp.dot(readout_matrix, hidden_activations.T, preferred_element_type=jnp.float32)).astype(jnp.bfloat16)
            return (predicted_states, hidden_activations)
        realization_prediction, realization_hidden = lax.map(realization_sweep, (scaling_factors, shift_terms_list))
        prediction_results.append(realization_prediction)
        complete_quantities = realization_prediction.astype(jnp.float32)
        truth = target[sample].astype(jnp.float32)
        to_truth = jnp.sqrt(lax.optimization_barrier(jnp.sum((complete_quantities - truth) ** 2, axis=(1, 2))) + EPSILON)

        def pair_row(other_row):
            return lax.optimization_barrier(jnp.sum((other_row - complete_quantities) ** 2, axis=(1, 2)))
        pair_dist = jnp.sqrt(lax.map(pair_row, complete_quantities) + EPSILON)
        sample_score = jnp.sum(to_truth) / MEMBERS - jnp.sum(pair_dist * pair_mask) / (2.0 * MEMBERS * MEMBERS)
        score_sum = score_sum + sample_score
        truth_pull = 1.0 / (MEMBERS * to_truth)
        pair_pull = pair_mask / (MEMBERS * MEMBERS * pair_dist)
        slope_bf = (truth_pull[:, None, None] * (complete_quantities - truth) - lax.optimization_barrier(jnp.sum(pair_pull, axis=1))[:, None, None] * complete_quantities + jnp.einsum('mn,nvg->mvg', pair_pull, complete_quantities, precision=lax.Precision.HIGHEST)).astype(jnp.bfloat16)
        for member_index in range(MEMBERS):
            gradient = gradient + jnp.dot(slope_bf[member_index], realization_hidden[member_index], preferred_element_type=jnp.float32)
    prediction_per_realization = jnp.stack(prediction_results, axis=0)
    objective_mean = score_sum / (SAMPLES * jnp.sqrt(jnp.float32(V * GRID)))
    unit_descent_slope = gradient / jnp.sqrt(jnp.mean(gradient * gradient) + EPSILON)
    return (prediction_per_realization, objective_mean, unit_descent_slope)
```

```python
import functools

import jax
import jax.numpy as jnp
from jax import lax
from jax.experimental import pallas as pl
from jax.experimental.pallas import tpu as pltpu
from jax.sharding import PartitionSpec as P

HEADS = 12
HD = 64
WIN = 64
K_ENC = 4
K_DEC = 3
EPSILON = 1e-06
LANES = 128
GROUP = 4
LOG2E = 1.4426950408889634

F32 = jnp.float32
BF16 = jnp.bfloat16

VMEM = pl.BlockSpec(memory_space=pltpu.VMEM)
SMEM = pl.BlockSpec(memory_space=pltpu.SMEM)
NT = (((1,), (1,)), ((), ()))


def dot(a, b):
    return jnp.dot(a, b, preferred_element_type=F32)


def dot_nt(a, b):
    return lax.dot_general(a, b, NT, preferred_element_type=F32)


def call(kernel, outs, args, specs=None, scratch=()):
    many = isinstance(outs, (tuple, list))
    return pl.pallas_call(
        kernel,
        out_shape=outs,
        in_specs=[VMEM] * len(args) if specs is None else specs,
        out_specs=[VMEM] * len(outs) if many else VMEM,
        scratch_shapes=list(scratch),
    )(*args)


def counts_of(index, targets):
    rows = index.shape[0]
    local = lax.rem(index, jnp.int32(targets))
    positions = lax.broadcasted_iota(jnp.int32, (rows, targets), 1)
    counts = (local[:, 0:1] == positions).astype(F32)
    for column in range(1, index.shape[1]):
        counts = counts + (local[:, column : column + 1] == positions).astype(F32)
    return counts.astype(BF16)


def pool_kernel(enc_ref, grid_ref, pooled_ref):
    counts = counts_of(enc_ref[...], grid_ref.shape[1])
    pooled_ref[...] = dot_nt(counts, grid_ref[...]) * (1.0 / K_ENC)


def in_parts(values):
    high = values.astype(BF16)
    rest = values - high.astype(F32)
    mid = rest.astype(BF16)
    low = (rest - mid.astype(F32)).astype(BF16)
    return high, mid, low


def states_kernel(left_ref, own_ref, right_ref, w_in_ref, dec_ref, states_ref, normed_ref, counts_ref):
    tok = own_ref.shape[0]
    w_in = w_in_ref[...]
    for slot, ref in enumerate((left_ref, own_ref, right_ref)):
        high, mid, low = in_parts(ref[...])
        states = dot(high, w_in) + (dot(mid, w_in) + dot(low, w_in))
        if slot == 1:
            states_ref[...] = states
        centre = states - jnp.mean(states, axis=-1, keepdims=True)
        spread = jnp.mean(centre * centre, axis=-1, keepdims=True)
        normed_ref[slot * tok : (slot + 1) * tok, :] = centre / jnp.sqrt(spread + EPSILON)
    counts = counts_of(dec_ref[...], tok)
    counts_ref[:, :tok] = counts
    counts_ref[:, tok:] = counts


def member_kernel(
    member,
    win_ref,
    gain_ref,
    shift_ref,
    normed_ref,
    states_ref,
    counts_ref,
    grid_ref,
    w_qkv_ref,
    w_o_ref,
    readout_ref,
    x_ref,
    feat_ref,
    kv_ref,
    att_ref,
):
    tok, d = states_ref.shape
    wins = tok // WIN
    wide = GROUP * HD
    inputs = (
        normed_ref[...] * gain_ref[member : member + 1, :] + shift_ref[member : member + 1, :]
    ).astype(BF16)
    kv_ref[...] = dot(inputs, w_qkv_ref[:, d:]).astype(BF16)
    queries = dot(inputs[tok : 2 * tok], w_qkv_ref[:, :d]).astype(BF16)
    head_of = lax.broadcasted_iota(jnp.int32, (WIN, wide), 1) // HD
    for w in range(wins):
        starts = [(wins + w) * WIN]
        for j in range(3):
            starts.append(pl.multiple_of(win_ref[w * 3 + j], WIN))
        for g in range(HEADS // GROUP):
            lo = g * wide
            q = queries[w * WIN : (w + 1) * WIN, lo : lo + wide]
            zero = jnp.zeros_like(q)
            spread = jnp.concatenate([jnp.where(head_of == h, q, zero) for h in range(GROUP)], axis=0)
            keys = jnp.concatenate([kv_ref[pl.ds(s, WIN), lo : lo + wide] for s in starts], axis=0)
            values = jnp.concatenate(
                [kv_ref[pl.ds(s, WIN), d + lo : d + lo + wide] for s in starts], axis=0
            )
            scores = dot_nt(spread, keys) * (HD ** (-0.5) * LOG2E)
            top = jnp.max(scores, axis=-1, keepdims=True)
            weights = jnp.exp2(scores - top)
            weights = weights * (1.0 / jnp.sum(weights, axis=-1, keepdims=True))
            mixed = dot(weights.astype(BF16), values)
            out = mixed[:WIN]
            for h in range(1, GROUP):
                out = jnp.where(head_of == h, mixed[h * WIN : (h + 1) * WIN], out)
            att_ref[w * WIN : (w + 1) * WIN, lo : lo + wide] = out.astype(BF16)
    updated = states_ref[...] + dot(att_ref[...], w_o_ref[...])
    high = updated.astype(BF16)
    low = (updated - high.astype(F32)).astype(BF16)
    features = (dot(counts_ref[...], jnp.concatenate([high, low], axis=0)) / K_DEC).astype(BF16)
    feat_ref[...] = features
    x_ref[...] = (grid_ref[...].astype(F32) + dot_nt(readout_ref[...], features)).astype(BF16)


def pair_list(own, other):
    pairs = [(i, j) for i in range(own) for j in range(i + 1, own)]
    cross = [(i, own + j) for i in range(own) for j in range(other)]
    return pairs, cross


def stats_kernel(members, target_ref, *refs):
    out_ref = refs[-1]
    xs = [r[...].astype(F32) for r in refs[:-1]]
    truth = target_ref[...].astype(F32)
    pairs, cross = pair_list(members, len(xs) - members)
    rows = []

    def lane_sums(diff):
        col = jnp.sum(diff * diff, axis=0, keepdims=True)
        total = col[:, :LANES]
        for c in range(1, col.shape[1] // LANES):
            total = total + col[:, c * LANES : (c + 1) * LANES]
        return total

    for i in range(members):
        rows.append(lane_sums(xs[i] - truth))
    for i, j in pairs + cross:
        rows.append(lane_sums(xs[i] - xs[j]))
    row_id = lax.broadcasted_iota(jnp.int32, (32, LANES), 0)
    lane_id = lax.broadcasted_iota(jnp.int32, (32, LANES), 1)
    table = jnp.zeros((32, LANES), F32)
    for k, row in enumerate(rows):
        table = jnp.where(row_id == k, row, table)
    sums = jnp.sum(table, axis=1, keepdims=True)
    line = jnp.sum(jnp.where(row_id == lane_id, sums, 0.0), axis=0, keepdims=True)
    out_ref[...] = jnp.broadcast_to(line[None], out_ref.shape)


def slope_kernel(members, members_all, peers, stat_ref, target_ref, *refs):
    xs = [r[...] for r in refs[: 2 * members]]
    feats = refs[2 * members : 3 * members]
    pred_ref, grad_ref, score_ref, pack_ref = refs[3 * members :]
    xf = [x.astype(F32) for x in xs]
    truth = target_ref[...].astype(F32)
    pairs, cross = pair_list(members, members)
    total = jnp.sum(stat_ref[...].reshape(stat_ref.shape[0], LANES), axis=0, keepdims=True)
    dist = jnp.sqrt(total + EPSILON)
    lane = lax.broadcasted_iota(jnp.int32, (1, LANES), 1)
    first_cross = members + len(pairs)
    end = first_cross + len(cross)
    m = float(members_all)
    share = jnp.where(
        lane < members,
        1.0 / m,
        jnp.where(lane < first_cross, -1.0 / (m * m), jnp.where(lane < end, -0.5 / (m * m), 0.0)),
    )
    score = jnp.sum(dist * share, axis=1, keepdims=True)
    score_ref[...] = jnp.broadcast_to(score, score_ref.shape)
    pull = 1.0 / (jnp.where(lane < members, m, m * m) * dist)
    coef = {}
    for k, (i, j) in enumerate(pairs + cross):
        value = pull[:, members + k : members + k + 1]
        coef[i, j] = value
        coef[j, i] = value
    acc = None
    for i in range(members):
        pred_ref[i] = xs[i]
        slope = pull[:, i : i + 1] * (xf[i] - truth)
        for j in range(2 * members):
            if j != i:
                slope = slope + coef[i, j] * (xf[j] - xf[i])
        part = dot(slope.astype(BF16), feats[i][...])
        acc = part if acc is None else acc + part
    v, d = acc.shape
    pack_ref[...] = jnp.zeros_like(pack_ref)
    for c in range(d // LANES):
        pack_ref[c * v : (c + 1) * v, :] = acc[:, c * LANES : (c + 1) * LANES]
    grad_ref[...] = pack_ref[...].astype(BF16).reshape(grad_ref.shape)


def share_kernel(recv_ref, score_ref, out_ref):
    rows = recv_ref.shape[1]
    total = jnp.sum(recv_ref[...].astype(F32), axis=0)
    both = jnp.concatenate([total, score_ref[...]], axis=0)
    out_ref[...] = jnp.broadcast_to(both[None], out_ref.shape)


def spread_kernel(scale, recv_ref, out_ref, score_ref):
    rows = out_ref.shape[1]
    total = jnp.sum(recv_ref[...], axis=0)
    out_ref[...] = jnp.broadcast_to(total[:rows][None], out_ref.shape)
    score_ref[...] = total[rows:] * scale


def final_kernel(recv_ref, out_ref, pack_ref):
    v, d = out_ref.shape
    pack_ref[...] = recv_ref[...].reshape(pack_ref.shape)
    grad = pack_ref[...]
    square = jnp.sum(jnp.sum(grad * grad, axis=0, keepdims=True), axis=1, keepdims=True)
    scale = 1.0 / jnp.sqrt(square / (v * d) + EPSILON)
    for c in range(d // LANES):
        out_ref[:, c * LANES : (c + 1) * LANES] = pack_ref[c * v : (c + 1) * v, :] * scale


def exchange(blocks, axis):
    return lax.all_to_all(blocks, axis, split_axis=0, concat_axis=0, tiled=True)


def body(
    grid_in,
    target,
    noise,
    neighbours,
    enc_index,
    dec_index,
    w_in,
    w_gamma,
    w_beta,
    w_qkv,
    w_o,
    readout_matrix,
):
    tok = enc_index.shape[0]
    points = dec_index.shape[0]
    d = w_o.shape[0]
    members = noise.shape[1]
    v = grid_in.shape[1]
    space = lax.axis_size("space")
    grid = grid_in[0]
    truth = target[0]
    shape = jax.ShapeDtypeStruct

    pooled = call(pool_kernel, shape((tok, v), F32), (enc_index, grid))
    up = [(i, (i + 1) % space) for i in range(space)]
    down = [((i + 1) % space, i) for i in range(space)]
    from_left = lax.ppermute(pooled, "space", up)
    from_right = lax.ppermute(pooled, "space", down)

    gain = 1.0 + jnp.dot(noise[0], w_gamma, precision=lax.Precision.HIGHEST)
    shift = jnp.dot(noise[0], w_beta, precision=lax.Precision.HIGHEST)

    per_dev = tok // WIN
    local_ids = jnp.arange(per_dev, dtype=jnp.int32)[:, None]
    first = lax.axis_index("space") * per_dev
    reach = (neighbours - first - local_ids + 2) % (per_dev * space) + local_ids
    starts = (reach * WIN).reshape(-1)

    states, normed, counts = call(
        states_kernel,
        (shape((tok, d), F32), shape((3 * tok, d), F32), shape((points, 2 * tok), BF16)),
        (from_left, pooled, from_right, w_in, dec_index),
    )
    own, feats = [], []
    for m in range(members):
        x, f = call(
            functools.partial(member_kernel, m),
            (shape((v, points), BF16), shape((points, d), BF16)),
            (starts, gain, shift, normed, states, counts, grid, w_qkv, w_o, readout_matrix),
            specs=[SMEM] + [VMEM] * 9,
            scratch=(pltpu.VMEM((3 * tok, 2 * d), BF16), pltpu.VMEM((tok, d), BF16)),
        )
        own.append(x)
        feats.append(f)
    other = [lax.ppermute(x, "member", [(0, 1), (1, 0)]) for x in own]

    members_all = members * lax.axis_size("member")
    stats = call(
        functools.partial(stats_kernel, members), shape((space, 1, LANES), F32), (truth, *own, *other)
    )
    stats = exchange(stats, "space")
    rows = -(-v * d // (LANES * space * 8)) * 8
    pred, grad, score = call(
        functools.partial(slope_kernel, members, members_all, space),
        (shape((members, v, points), BF16), shape((space, rows, LANES), BF16), shape((8, LANES), F32)),
        (stats, truth, *own, *other, *feats),
        scratch=(pltpu.VMEM((space * rows, LANES), F32),),
    )
    grad = exchange(grad, "space")
    peers = lax.axis_size("dp") * lax.axis_size("member")
    share = call(share_kernel, shape((peers, rows + 8, LANES), F32), (grad, score))
    share = exchange(share, ("dp", "member"))
    scale = 1.0 / (lax.axis_size("dp") * (v * points * space) ** 0.5)
    spread, objective = call(
        functools.partial(spread_kernel, scale),
        (shape((space, rows, LANES), F32), shape((8, LANES), F32)),
        (share,),
    )
    spread = exchange(spread, "space")
    unit = call(
        final_kernel, shape((v, d), F32), (spread,), scratch=(pltpu.VMEM((space * rows, LANES), F32),)
    )
    return (pred[None], objective[0, 0], unit)


def solution(mesh):
    in_specs = (
        P("dp", None, "space"),
        P("dp", None, "space"),
        P("dp", "member", None),
        P("space", None),
        P("space", None),
        P("space", None),
        P(),
        P(),
        P(),
        P(),
        P(),
        P(),
    )
    out_specs = (P("dp", "member", None, "space"), P(), P())
    return jax.shard_map(body, mesh=mesh, in_specs=in_specs, out_specs=out_specs, check_vma=False)
```

```python
import functools

import jax
import jax.numpy as jnp
from jax import lax
from jax.experimental import pallas as pl
from jax.experimental.pallas import tpu as pltpu
from jax.sharding import PartitionSpec as P

HEADS = 12
HD = 64
WIN = 64
K_ENC = 4
K_DEC = 3
EPSILON = 1e-06
LANES = 128
GROUP = 4
LOG2E = 1.4426950408889634

F32 = jnp.float32
BF16 = jnp.bfloat16

VMEM = pl.BlockSpec(memory_space=pltpu.VMEM)
SMEM = pl.BlockSpec(memory_space=pltpu.SMEM)
NT = (((1,), (1,)), ((), ()))


def dot(a, b):
    return jnp.dot(a, b, preferred_element_type=F32)


def dot_nt(a, b):
    return lax.dot_general(a, b, NT, preferred_element_type=F32)


def call(kernel, outs, args, smem=(), scratch=(), limit=24):
    many = isinstance(outs, list)
    kept = [
        a if i in smem else pltpu.with_memory_space_constraint(a, pltpu.VMEM) for i, a in enumerate(args)
    ]
    return pl.pallas_call(
        kernel,
        out_shape=outs,
        in_specs=[SMEM if i in smem else VMEM for i in range(len(args))],
        out_specs=[VMEM] * len(outs) if many else VMEM,
        scratch_shapes=list(scratch),
        compiler_params=pltpu.CompilerParams(vmem_limit_bytes=limit << 20),
    )(*kept)


def counts_of(index_rows, targets):
    many = index_rows.shape[1]
    local = lax.rem(index_rows, jnp.int32(targets))
    positions = lax.broadcasted_iota(jnp.int32, (targets, many), 0)
    counts = (local[0:1, :] == positions).astype(F32)
    for row in range(1, index_rows.shape[0]):
        counts = counts + (local[row : row + 1, :] == positions).astype(F32)
    return counts


def pool_kernel(enc_ref, grid_ref, pooled_ref):
    counts = counts_of(enc_ref[...], grid_ref.shape[1]).astype(BF16)
    pooled_ref[...] = dot(grid_ref[...], counts) * (1.0 / K_ENC)


def states_of(pooled, w_in):
    values = pooled.T
    high = values.astype(BF16)
    rest = values - high.astype(F32)
    mid = rest.astype(BF16)
    low = (rest - mid.astype(F32)).astype(BF16)
    return dot(high, w_in) + (dot(mid, w_in) + dot(low, w_in))


def normed_of(states):
    centre = states - jnp.mean(states, axis=-1, keepdims=True)
    spread = jnp.mean(centre * centre, axis=-1, keepdims=True)
    return centre / jnp.sqrt(spread + EPSILON)


def own_kernel(
    pooled_ref,
    w_in_ref,
    noise_ref,
    w_gamma_ref,
    w_beta_ref,
    w_qkv_ref,
    dec_ref,
    states_ref,
    gain_ref,
    shift_ref,
    project_ref,
    counts_ref,
    inputs_ref,
):
    tok, d = states_ref.shape
    members = noise_ref.shape[0]
    gain = 1.0 + jnp.dot(noise_ref[...], w_gamma_ref[...], precision=lax.Precision.HIGHEST)
    shift = jnp.dot(noise_ref[...], w_beta_ref[...], precision=lax.Precision.HIGHEST)
    gain_ref[...] = gain
    shift_ref[...] = shift
    states = states_of(pooled_ref[...], w_in_ref[...])
    states_ref[...] = states
    normed = normed_of(states)
    for m in range(members):
        inputs_ref[m * tok : (m + 1) * tok, :] = (normed * gain[m : m + 1] + shift[m : m + 1]).astype(BF16)
    for c in range(3):
        part = dot(inputs_ref[...], w_qkv_ref[:, c * d : (c + 1) * d])
        project_ref[:, c * d : (c + 1) * d] = part.astype(BF16)
    counts = counts_of(dec_ref[...], tok).T.astype(BF16)
    counts_ref[:, :tok] = counts
    counts_ref[:, tok:] = counts


def members_kernel(
    nbr_ref,
    left_ref,
    right_ref,
    w_in_ref,
    gain_ref,
    shift_ref,
    project_ref,
    states_ref,
    counts_ref,
    grid_ref,
    w_qkv_ref,
    w_o_ref,
    readout_ref,
    x_ref,
    feat_ref,
    edge_ref,
    kv_ref,
    att_ref,
    upd_ref,
):
    tok, d = states_ref.shape
    members = gain_ref.shape[0]
    wins = tok // WIN
    wide = GROUP * HD
    windows = wins * lax.axis_size("space")
    first = lax.axis_index("space") * wins
    for slot, ref in enumerate((left_ref, right_ref)):
        normed = normed_of(states_of(ref[...], w_in_ref[...]))
        for m in range(members):
            row = (2 * m + slot) * tok
            edge_ref[row : row + tok, :] = (
                normed * gain_ref[m : m + 1, :] + shift_ref[m : m + 1, :]
            ).astype(BF16)
    for c in range(2):
        lo = c * d
        part = dot(edge_ref[...], w_qkv_ref[:, d + lo : d + lo + d]).astype(BF16)
        for m in range(members):
            kv_ref[m, :tok, lo : lo + d] = part[2 * m * tok : (2 * m + 1) * tok]
            kv_ref[m, tok : 2 * tok, lo : lo + d] = project_ref[m * tok : (m + 1) * tok, d + lo : d + lo + d]
            kv_ref[m, 2 * tok :, lo : lo + d] = part[(2 * m + 1) * tok : (2 * m + 2) * tok]
    head_of = lax.broadcasted_iota(jnp.int32, (WIN, wide), 1) // HD

    def attend(m, carry):
        for w in range(wins):
            starts = [(wins + w) * WIN]
            for j in range(nbr_ref.shape[1]):
                reach = lax.rem(nbr_ref[w, j] - first - w + 2 + windows, windows) + w
                starts.append(pl.multiple_of(reach * WIN, WIN))
            row = pl.multiple_of(m * tok + w * WIN, WIN)
            for g in range(HEADS // GROUP):
                lo = g * wide
                q = project_ref[pl.ds(row, WIN), lo : lo + wide]
                zero = jnp.zeros_like(q)
                spread = jnp.concatenate([jnp.where(head_of == h, q, zero) for h in range(GROUP)], axis=0)
                keys = jnp.concatenate([kv_ref[m, pl.ds(s, WIN), lo : lo + wide] for s in starts], axis=0)
                values = jnp.concatenate(
                    [kv_ref[m, pl.ds(s, WIN), d + lo : d + lo + wide] for s in starts], axis=0
                )
                scores = dot_nt(spread, keys) * (HD ** (-0.5) * LOG2E)
                top = jnp.max(scores, axis=-1, keepdims=True)
                weights = jnp.exp2(scores - top)
                weights = weights * (1.0 / jnp.sum(weights, axis=-1, keepdims=True))
                mixed = dot(weights.astype(BF16), values)
                out = mixed[:WIN]
                for h in range(1, GROUP):
                    out = jnp.where(head_of == h, mixed[h * WIN : (h + 1) * WIN], out)
                att_ref[pl.ds(row, WIN), lo : lo + wide] = out.astype(BF16)
        return carry

    lax.fori_loop(0, members, attend, 0)
    mixed = dot(att_ref[...], w_o_ref[...])
    for m in range(members):
        updated = states_ref[...] + mixed[m * tok : (m + 1) * tok]
        high = updated.astype(BF16)
        upd_ref[m, :tok, :] = high
        upd_ref[m, tok:, :] = (updated - high.astype(F32)).astype(BF16)

    def decode(m, carry):
        features = (dot(counts_ref[...], upd_ref[m]) / K_DEC).astype(BF16)
        feat_ref[m] = features
        x_ref[m] = (grid_ref[...].astype(F32) + dot_nt(readout_ref[...], features)).astype(BF16)
        return carry

    lax.fori_loop(0, members, decode, 0)


def pair_list(own, other):
    pairs = [(i, j) for i in range(own) for j in range(i + 1, own)]
    cross = [(i, own + j) for i in range(own) for j in range(other)]
    return pairs, cross


def stats_kernel(members, target_ref, *refs):
    out_ref = refs[-1]
    xs = [r[i].astype(F32) for r in refs[:-1] for i in range(members)]
    truth = target_ref[...].astype(F32)
    pairs, cross = pair_list(members, len(xs) - members)
    rows = []

    def lane_sums(diff):
        col = jnp.sum(diff * diff, axis=0, keepdims=True)
        total = col[:, :LANES]
        for c in range(1, col.shape[1] // LANES):
            total = total + col[:, c * LANES : (c + 1) * LANES]
        return total

    for i in range(members):
        rows.append(lane_sums(xs[i] - truth))
    for i, j in pairs + cross:
        rows.append(lane_sums(xs[i] - xs[j]))
    row_id = lax.broadcasted_iota(jnp.int32, (32, LANES), 0)
    lane_id = lax.broadcasted_iota(jnp.int32, (32, LANES), 1)
    table = jnp.zeros((32, LANES), F32)
    for k, row in enumerate(rows):
        table = jnp.where(row_id == k, row, table)
    sums = jnp.sum(table, axis=1, keepdims=True)
    line = jnp.sum(jnp.where(row_id == lane_id, sums, 0.0), axis=0, keepdims=True)
    out_ref[...] = jnp.broadcast_to(line[None], out_ref.shape)


def slope_kernel(
    members_all, stat_ref, target_ref, own_ref, other_ref, feat_ref, pred_ref, grad_ref, score_ref, pack_ref
):
    members = own_ref.shape[0]
    xs = [r[i] for r in (own_ref, other_ref) for i in range(members)]
    xf = [x.astype(F32) for x in xs]
    truth = target_ref[...].astype(F32)
    pairs, cross = pair_list(members, members)
    total = jnp.sum(stat_ref[...].reshape(stat_ref.shape[0], LANES), axis=0, keepdims=True)
    dist = jnp.sqrt(total + EPSILON)
    lane = lax.broadcasted_iota(jnp.int32, (1, LANES), 1)
    first_cross = members + len(pairs)
    end = first_cross + len(cross)
    m = float(members_all)
    share = jnp.where(
        lane < members,
        1.0 / m,
        jnp.where(lane < first_cross, -1.0 / (m * m), jnp.where(lane < end, -0.5 / (m * m), 0.0)),
    )
    score = jnp.sum(dist * share, axis=1, keepdims=True)
    score_ref[...] = jnp.broadcast_to(score, score_ref.shape)
    pull = 1.0 / (jnp.where(lane < members, m, m * m) * dist)
    coef = {}
    for k, (i, j) in enumerate(pairs + cross):
        value = pull[:, members + k : members + k + 1]
        coef[i, j] = value
        coef[j, i] = value
    acc = None
    for i in range(members):
        pred_ref[i] = xs[i]
        slope = pull[:, i : i + 1] * (xf[i] - truth)
        for j in range(2 * members):
            if j != i:
                slope = slope + coef[i, j] * (xf[j] - xf[i])
        part = dot(slope.astype(BF16), feat_ref[i])
        acc = part if acc is None else acc + part
    v, d = acc.shape
    pack_ref[...] = jnp.zeros_like(pack_ref)
    for c in range(d // LANES):
        pack_ref[c * v : (c + 1) * v, :] = acc[:, c * LANES : (c + 1) * LANES]
    grad_ref[...] = pack_ref[...].astype(BF16).reshape(grad_ref.shape)


def share_kernel(recv_ref, score_ref, out_ref):
    rows = recv_ref.shape[1]
    total = jnp.sum(recv_ref[...].astype(F32), axis=0)
    both = jnp.concatenate([total, score_ref[...]], axis=0)
    out_ref[...] = jnp.broadcast_to(both[None], out_ref.shape)


def spread_kernel(scale, recv_ref, out_ref, score_ref):
    rows = out_ref.shape[1]
    total = jnp.sum(recv_ref[...], axis=0)
    out_ref[...] = jnp.broadcast_to(total[:rows][None], out_ref.shape)
    score_ref[...] = total[rows:] * scale


def final_kernel(recv_ref, out_ref, pack_ref):
    v, d = out_ref.shape
    pack_ref[...] = recv_ref[...].reshape(pack_ref.shape)
    grad = pack_ref[...]
    square = jnp.sum(jnp.sum(grad * grad, axis=0, keepdims=True), axis=1, keepdims=True)
    scale = 1.0 / jnp.sqrt(square / (v * d) + EPSILON)
    for c in range(d // LANES):
        out_ref[:, c * LANES : (c + 1) * LANES] = pack_ref[c * v : (c + 1) * v, :] * scale


def exchange(blocks, axis):
    return lax.all_to_all(blocks, axis, split_axis=0, concat_axis=0, tiled=True)


def body(
    grid_in,
    target,
    noise,
    neighbours,
    enc_index,
    dec_index,
    w_in,
    w_gamma,
    w_beta,
    w_qkv,
    w_o,
    readout_matrix,
):
    tok = enc_index.shape[0]
    points = dec_index.shape[0]
    d = w_o.shape[0]
    members = noise.shape[1]
    v = grid_in.shape[1]
    space = lax.axis_size("space")
    grid = grid_in[0]
    truth = target[0]

    pooled = call(pool_kernel, pltpu.VMEM((v, tok), F32), (enc_index.T, grid))
    up = [(i, (i + 1) % space) for i in range(space)]
    down = [((i + 1) % space, i) for i in range(space)]
    from_left = lax.ppermute(pooled, "space", up)
    from_right = lax.ppermute(pooled, "space", down)
    states, gain, shift, project, counts = call(
        own_kernel,
        [
            pltpu.VMEM((tok, d), F32),
            pltpu.VMEM((members, d), F32),
            pltpu.VMEM((members, d), F32),
            pltpu.VMEM((members * tok, 3 * d), BF16),
            pltpu.VMEM((points, 2 * tok), BF16),
        ],
        (pooled, w_in, noise[0], w_gamma, w_beta, w_qkv, dec_index.T),
        scratch=(pltpu.VMEM((members * tok, d), BF16),),
    )
    own, feats = call(
        members_kernel,
        [pltpu.VMEM((members, v, points), BF16), pltpu.VMEM((members, points, d), BF16)],
        (
            neighbours,
            from_left,
            from_right,
            w_in,
            gain,
            shift,
            project,
            states,
            counts,
            grid,
            w_qkv,
            w_o,
            readout_matrix,
        ),
        smem=(0,),
        scratch=(
            pltpu.VMEM((2 * members * tok, d), BF16),
            pltpu.VMEM((members, 3 * tok, 2 * d), BF16),
            pltpu.VMEM((members * tok, d), BF16),
            pltpu.VMEM((members, 2 * tok, d), BF16),
        ),
    )
    other = lax.ppermute(own, "member", [(0, 1), (1, 0)])

    members_all = members * lax.axis_size("member")
    stats = call(
        functools.partial(stats_kernel, members), pltpu.VMEM((space, 1, LANES), F32), (truth, own, other)
    )
    stats = exchange(stats, "space")
    rows = -(-v * d // (LANES * space * 8)) * 8
    pred, grad, score = call(
        functools.partial(slope_kernel, members_all),
        [
            jax.ShapeDtypeStruct((members, v, points), BF16),
            pltpu.VMEM((space, rows, LANES), BF16),
            pltpu.VMEM((8, LANES), F32),
        ],
        (stats, truth, own, other, feats),
        scratch=(pltpu.VMEM((space * rows, LANES), F32),),
    )
    grad = exchange(grad, "space")
    peers = lax.axis_size("dp") * lax.axis_size("member")
    share = call(share_kernel, pltpu.VMEM((peers, rows + 8, LANES), F32), (grad, score))
    share = exchange(share, ("dp", "member"))
    scale = 1.0 / (lax.axis_size("dp") * (v * points * space) ** 0.5)
    spread, objective = call(
        functools.partial(spread_kernel, scale),
        [pltpu.VMEM((space, rows, LANES), F32), pltpu.VMEM((8, LANES), F32)],
        (share,),
    )
    spread = exchange(spread, "space")
    unit = call(
        final_kernel,
        jax.ShapeDtypeStruct((v, d), F32),
        (spread,),
        scratch=(pltpu.VMEM((space * rows, LANES), F32),),
    )
    return (pred[None], objective[0, 0], unit)


def solution(mesh):
    in_specs = (
        P("dp", None, "space"),
        P("dp", None, "space"),
        P("dp", "member", None),
        P("space", None),
        P("space", None),
        P("space", None),
        P(),
        P(),
        P(),
        P(),
        P(),
        P(),
    )
    out_specs = (P("dp", "member", None, "space"), P(), P())
    return jax.shard_map(body, mesh=mesh, in_specs=in_specs, out_specs=out_specs, check_vma=False)
```

```python
import functools

import jax
import jax.numpy as jnp
from jax import lax
from jax.experimental import pallas as pl
from jax.experimental.pallas import tpu as pltpu
from jax.sharding import PartitionSpec as P

HEADS = 12
HD = 64
WIN = 64
K_ENC = 4
K_DEC = 3
EPSILON = 1e-06
LANES = 128
GROUP = 4
LOG2E = 1.4426950408889634

F32 = jnp.float32
BF16 = jnp.bfloat16

VMEM = pl.BlockSpec(memory_space=pltpu.VMEM)
SMEM = pl.BlockSpec(memory_space=pltpu.SMEM)
NT = (((1,), (1,)), ((), ()))


def dot(a, b):
    return jnp.dot(a, b, preferred_element_type=F32)


def dot_nt(a, b):
    return lax.dot_general(a, b, NT, preferred_element_type=F32)


def call(kernel, outs, args, smem=(), scratch=(), limit=24, work=0):
    many = isinstance(outs, list)
    kept = [
        a if i in smem else pltpu.with_memory_space_constraint(a, pltpu.VMEM) for i, a in enumerate(args)
    ]
    return pl.pallas_call(
        kernel,
        out_shape=outs,
        in_specs=[SMEM if i in smem else VMEM for i in range(len(args))],
        out_specs=[VMEM] * len(outs) if many else VMEM,
        scratch_shapes=list(scratch),
        compiler_params=pltpu.CompilerParams(vmem_limit_bytes=limit << 20),
        cost_estimate=pl.CostEstimate(flops=work, transcendentals=0, bytes_accessed=work // 100),
    )(*kept)


def counts_of(index_rows, targets):
    many = index_rows.shape[1]
    local = lax.rem(index_rows, jnp.int32(targets))
    positions = lax.broadcasted_iota(jnp.int32, (targets, many), 0)
    counts = (local[0:1, :] == positions).astype(F32)
    for row in range(1, index_rows.shape[0]):
        counts = counts + (local[row : row + 1, :] == positions).astype(F32)
    return counts


def pool_kernel(enc_ref, grid_ref, pooled_ref):
    counts = counts_of(enc_ref[...], grid_ref.shape[1]).astype(BF16)
    pooled_ref[...] = dot(grid_ref[...], counts) * (1.0 / K_ENC)


def states_of(pooled, w_in):
    values = pooled.T
    high = values.astype(BF16)
    rest = values - high.astype(F32)
    mid = rest.astype(BF16)
    low = (rest - mid.astype(F32)).astype(BF16)
    return dot(high, w_in) + (dot(mid, w_in) + dot(low, w_in))


def normed_of(states):
    centre = states - jnp.mean(states, axis=-1, keepdims=True)
    spread = jnp.mean(centre * centre, axis=-1, keepdims=True)
    return centre / jnp.sqrt(spread + EPSILON)


def own_kernel(
    pooled_ref,
    w_in_ref,
    noise_ref,
    w_gamma_ref,
    w_beta_ref,
    w_qkv_ref,
    dec_ref,
    states_ref,
    gain_ref,
    shift_ref,
    project_ref,
    counts_ref,
    inputs_ref,
):
    tok, d = states_ref.shape
    members = noise_ref.shape[0]
    gain = 1.0 + jnp.dot(noise_ref[...], w_gamma_ref[...], precision=lax.Precision.HIGHEST)
    shift = jnp.dot(noise_ref[...], w_beta_ref[...], precision=lax.Precision.HIGHEST)
    gain_ref[...] = gain
    shift_ref[...] = shift
    states = states_of(pooled_ref[...], w_in_ref[...])
    states_ref[...] = states
    normed = normed_of(states)
    for m in range(members):
        inputs_ref[m * tok : (m + 1) * tok, :] = (normed * gain[m : m + 1] + shift[m : m + 1]).astype(BF16)
    for c in range(3):
        part = dot(inputs_ref[...], w_qkv_ref[:, c * d : (c + 1) * d])
        project_ref[:, c * d : (c + 1) * d] = part.astype(BF16)
    counts = counts_of(dec_ref[...], tok).T.astype(BF16)
    counts_ref[:, :tok] = counts
    counts_ref[:, tok:] = counts


def members_kernel(
    nbr_ref,
    left_ref,
    right_ref,
    w_in_ref,
    gain_ref,
    shift_ref,
    project_ref,
    states_ref,
    counts_ref,
    grid_ref,
    w_qkv_ref,
    w_o_ref,
    readout_ref,
    x_ref,
    ahead_ref,
    kept_ref,
    feat_ref,
    edge_ref,
    kv_ref,
    att_ref,
    upd_ref,
):
    tok, d = states_ref.shape
    members = gain_ref.shape[0]
    wins = tok // WIN
    wide = GROUP * HD
    windows = wins * lax.axis_size("space")
    first = lax.axis_index("space") * wins
    for slot, ref in enumerate((left_ref, right_ref)):
        normed = normed_of(states_of(ref[...], w_in_ref[...]))
        for m in range(members):
            row = (2 * m + slot) * tok
            edge_ref[row : row + tok, :] = (
                normed * gain_ref[m : m + 1, :] + shift_ref[m : m + 1, :]
            ).astype(BF16)
    for c in range(2):
        lo = c * d
        part = dot(edge_ref[...], w_qkv_ref[:, d + lo : d + lo + d]).astype(BF16)
        for m in range(members):
            kv_ref[m, :tok, lo : lo + d] = part[2 * m * tok : (2 * m + 1) * tok]
            kv_ref[m, tok : 2 * tok, lo : lo + d] = project_ref[m * tok : (m + 1) * tok, d + lo : d + lo + d]
            kv_ref[m, 2 * tok :, lo : lo + d] = part[(2 * m + 1) * tok : (2 * m + 2) * tok]
    head_of = lax.broadcasted_iota(jnp.int32, (WIN, wide), 1) // HD

    def attend(m, carry):
        for w in range(wins):
            starts = [(wins + w) * WIN]
            for j in range(nbr_ref.shape[1]):
                reach = lax.rem(nbr_ref[w, j] - first - w + 2 + windows, windows) + w
                starts.append(pl.multiple_of(reach * WIN, WIN))
            row = pl.multiple_of(m * tok + w * WIN, WIN)
            for g in range(HEADS // GROUP):
                lo = g * wide
                q = project_ref[pl.ds(row, WIN), lo : lo + wide]
                zero = jnp.zeros_like(q)
                spread = jnp.concatenate([jnp.where(head_of == h, q, zero) for h in range(GROUP)], axis=0)
                keys = jnp.concatenate([kv_ref[m, pl.ds(s, WIN), lo : lo + wide] for s in starts], axis=0)
                values = jnp.concatenate(
                    [kv_ref[m, pl.ds(s, WIN), d + lo : d + lo + wide] for s in starts], axis=0
                )
                scores = dot_nt(spread, keys) * (HD ** (-0.5) * LOG2E)
                top = jnp.max(scores, axis=-1, keepdims=True)
                weights = jnp.exp2(scores - top)
                weights = weights * (1.0 / jnp.sum(weights, axis=-1, keepdims=True))
                mixed = dot(weights.astype(BF16), values)
                out = mixed[:WIN]
                for h in range(1, GROUP):
                    out = jnp.where(head_of == h, mixed[h * WIN : (h + 1) * WIN], out)
                att_ref[pl.ds(row, WIN), lo : lo + wide] = out.astype(BF16)
        return carry

    lax.fori_loop(0, members, attend, 0)
    mixed = dot(att_ref[...], w_o_ref[...])
    for m in range(members):
        updated = states_ref[...] + mixed[m * tok : (m + 1) * tok]
        high = updated.astype(BF16)
        upd_ref[m, :tok, :] = high
        upd_ref[m, tok:, :] = (updated - high.astype(F32)).astype(BF16)

    second = lax.axis_index("member") == 1

    def decode(m, carry):
        features = (dot(counts_ref[...], upd_ref[m]) / K_DEC).astype(BF16)
        feat_ref[m] = features
        x = (grid_ref[...].astype(F32) + dot_nt(readout_ref[...], features)).astype(BF16)
        x_ref[m] = x
        half = x.shape[1] // 2
        ahead_ref[m] = jnp.where(second, x[:, :half], x[:, half:])
        kept_ref[m] = jnp.where(second, x[:, half:], x[:, :half])
        return carry

    lax.fori_loop(0, members, decode, 0)


def pair_list(count):
    return [(i, j) for i in range(count) for j in range(i + 1, count)]


def stats_kernel(target_ref, own_ref, other_ref, out_ref):
    members, _, half = own_ref.shape
    second = lax.axis_index("member") == 1
    xs = [jnp.where(second, other_ref[i], own_ref[i]).astype(F32) for i in range(members)]
    xs += [jnp.where(second, own_ref[i], other_ref[i]).astype(F32) for i in range(members)]
    truth = jnp.where(second, target_ref[:, half:], target_ref[:, :half]).astype(F32)

    def lane_sums(diff):
        col = jnp.sum(diff * diff, axis=0, keepdims=True)
        total = col[:, :LANES]
        for c in range(1, half // LANES):
            total = total + col[:, c * LANES : (c + 1) * LANES]
        return total

    rows = [lane_sums(x - truth) for x in xs]
    rows += [lane_sums(xs[i] - xs[j]) for i, j in pair_list(len(xs))]
    height = -(-len(rows) // 8) * 8
    row_id = lax.broadcasted_iota(jnp.int32, (height, LANES), 0)
    lane_id = lax.broadcasted_iota(jnp.int32, (height, LANES), 1)
    table = jnp.zeros((height, LANES), F32)
    for k, row in enumerate(rows):
        table = jnp.where(row_id == k, row, table)
    sums = jnp.sum(table, axis=1, keepdims=True)
    line = jnp.sum(jnp.where(row_id == lane_id, sums, 0.0), axis=0, keepdims=True)
    out_ref[...] = jnp.broadcast_to(line[None], out_ref.shape)


def slope_kernel(
    stat_ref, target_ref, own_ref, near_ref, far_ref, feat_ref, pred_ref, grad_ref, score_ref, pack_ref
):
    members = own_ref.shape[0]
    count = 2 * members
    second = lax.axis_index("member") == 1
    own = [own_ref[i] for i in range(members)]
    xf = [x.astype(F32) for x in own]
    for i in range(members):
        left = jnp.where(second, far_ref[i], near_ref[i])
        right = jnp.where(second, near_ref[i], far_ref[i])
        xf.append(jnp.concatenate([left, right], axis=1).astype(F32))
    truth = target_ref[...].astype(F32)
    pairs = pair_list(count)
    total = jnp.sum(stat_ref[...].reshape(stat_ref.shape[0], LANES), axis=0, keepdims=True)
    dist = jnp.sqrt(total + EPSILON)
    lane = lax.broadcasted_iota(jnp.int32, (1, LANES), 1)
    m = float(count)
    share = jnp.where(lane < count, 0.5 / m, jnp.where(lane < count + len(pairs), -0.5 / (m * m), 0.0))
    score = jnp.sum(dist * share, axis=1, keepdims=True)
    score_ref[...] = jnp.broadcast_to(score, score_ref.shape)
    pull = 1.0 / (jnp.where(lane < count, m, m * m) * dist)
    place = {}
    for k, (i, j) in enumerate(pairs):
        place[i, j] = place[j, i] = count + k

    def picked(first_lane, second_lane):
        return jnp.where(
            second, pull[:, second_lane : second_lane + 1], pull[:, first_lane : first_lane + 1]
        )

    acc = None
    for i in range(members):
        pred_ref[i] = own[i]
        slope = picked(i, members + i) * (xf[i] - truth)
        for j in range(count):
            if j != i:
                coef = picked(place[i, j], place[members + i, (members + j) % count])
                slope = slope + coef * (xf[j] - xf[i])
        part = dot(slope.astype(BF16), feat_ref[i])
        acc = part if acc is None else acc + part
    v, d = acc.shape
    pack_ref[...] = jnp.zeros_like(pack_ref)
    for c in range(d // LANES):
        pack_ref[c * v : (c + 1) * v, :] = acc[:, c * LANES : (c + 1) * LANES]
    grad_ref[...] = pack_ref[...].astype(BF16).reshape(grad_ref.shape)


def share_kernel(recv_ref, score_ref, out_ref):
    rows = recv_ref.shape[1]
    total = jnp.sum(recv_ref[...].astype(F32), axis=0)
    both = jnp.concatenate([total, score_ref[...]], axis=0)
    out_ref[...] = jnp.broadcast_to(both[None], out_ref.shape)


def spread_kernel(scale, recv_ref, out_ref, score_ref):
    rows = out_ref.shape[1]
    total = jnp.sum(recv_ref[...], axis=0)
    out_ref[...] = jnp.broadcast_to(total[:rows][None], out_ref.shape)
    score_ref[...] = total[rows:] * scale


def final_kernel(recv_ref, out_ref, pack_ref):
    v, d = out_ref.shape
    pack_ref[...] = recv_ref[...].reshape(pack_ref.shape)
    grad = pack_ref[...]
    square = jnp.sum(jnp.sum(grad * grad, axis=0, keepdims=True), axis=1, keepdims=True)
    scale = 1.0 / jnp.sqrt(square / (v * d) + EPSILON)
    for c in range(d // LANES):
        out_ref[:, c * LANES : (c + 1) * LANES] = pack_ref[c * v : (c + 1) * v, :] * scale


def exchange(blocks, axis):
    return lax.all_to_all(blocks, axis, split_axis=0, concat_axis=0, tiled=True)


def body(
    grid_in,
    target,
    noise,
    neighbours,
    enc_index,
    dec_index,
    w_in,
    w_gamma,
    w_beta,
    w_qkv,
    w_o,
    readout_matrix,
):
    tok = enc_index.shape[0]
    points = dec_index.shape[0]
    d = w_o.shape[0]
    members = noise.shape[1]
    v = grid_in.shape[1]
    space = lax.axis_size("space")
    grid = grid_in[0]
    truth = target[0]

    pooled = call(pool_kernel, pltpu.VMEM((v, tok), F32), (enc_index.T, grid), work=4 * 10**9)
    up = [(i, (i + 1) % space) for i in range(space)]
    down = [((i + 1) % space, i) for i in range(space)]
    from_left = lax.ppermute(pooled, "space", up)
    from_right = lax.ppermute(pooled, "space", down)
    states, gain, shift, project, counts = call(
        own_kernel,
        [
            pltpu.VMEM((tok, d), F32),
            pltpu.VMEM((members, d), F32),
            pltpu.VMEM((members, d), F32),
            pltpu.VMEM((members * tok, 3 * d), BF16),
            pltpu.VMEM((points, 2 * tok), BF16),
        ],
        (pooled, w_in, noise[0], w_gamma, w_beta, w_qkv, dec_index.T),
        scratch=(pltpu.VMEM((members * tok, d), BF16),),
        work=4 * 10**9,
    )
    half = pltpu.VMEM((members, v, points // 2), BF16)
    own, ahead, kept, feats = call(
        members_kernel,
        [pltpu.VMEM((members, v, points), BF16), half, half, pltpu.VMEM((members, points, d), BF16)],
        (
            neighbours,
            from_left,
            from_right,
            w_in,
            gain,
            shift,
            project,
            states,
            counts,
            grid,
            w_qkv,
            w_o,
            readout_matrix,
        ),
        smem=(0,),
        scratch=(
            pltpu.VMEM((2 * members * tok, d), BF16),
            pltpu.VMEM((members, 3 * tok, 2 * d), BF16),
            pltpu.VMEM((members * tok, d), BF16),
            pltpu.VMEM((members, 2 * tok, d), BF16),
        ),
        work=8 * 10**9,
    )
    near = lax.ppermute(ahead, "member", [(0, 1), (1, 0)])
    far = lax.ppermute(kept, "member", [(0, 1), (1, 0)])
    pair_space = space * lax.axis_size("member")
    stats = call(stats_kernel, pltpu.VMEM((pair_space, 1, LANES), F32), (truth, kept, near))
    stats = exchange(stats, ("member", "space"))
    rows = -(-v * d // (LANES * space * 8)) * 8
    pred, grad, score = call(
        slope_kernel,
        [
            jax.ShapeDtypeStruct((members, v, points), BF16),
            pltpu.VMEM((space, rows, LANES), BF16),
            pltpu.VMEM((8, LANES), F32),
        ],
        (stats, truth, own, near, far, feats),
        scratch=(pltpu.VMEM((space * rows, LANES), F32),),
    )
    grad = exchange(grad, "space")
    peers = lax.axis_size("dp") * lax.axis_size("member")
    share = call(share_kernel, pltpu.VMEM((peers, rows + 8, LANES), F32), (grad, score))
    share = exchange(share, ("dp", "member"))
    scale = 1.0 / (lax.axis_size("dp") * (v * points * space) ** 0.5)
    spread, objective = call(
        functools.partial(spread_kernel, scale),
        [pltpu.VMEM((space, rows, LANES), F32), pltpu.VMEM((8, LANES), F32)],
        (share,),
    )
    spread = exchange(spread, "space")
    unit = call(
        final_kernel,
        jax.ShapeDtypeStruct((v, d), F32),
        (spread,),
        scratch=(pltpu.VMEM((space * rows, LANES), F32),),
    )
    return (pred[None], objective[0, 0], unit)


def solution(mesh):
    in_specs = (
        P("dp", None, "space"),
        P("dp", None, "space"),
        P("dp", "member", None),
        P("space", None),
        P("space", None),
        P("space", None),
        P(),
        P(),
        P(),
        P(),
        P(),
        P(),
    )
    out_specs = (P("dp", "member", None, "space"), P(), P())
    return jax.shard_map(body, mesh=mesh, in_specs=in_specs, out_specs=out_specs, check_vma=False)
```

```python
import functools

import jax
import jax.numpy as jnp
from jax import lax
from jax.experimental import pallas as pl
from jax.experimental.pallas import tpu as pltpu
from jax.sharding import PartitionSpec as P

HEADS = 12
HD = 64
WIN = 64
K_ENC = 4
K_DEC = 3
EPSILON = 1e-06
LANES = 128
GROUP = 4
LOG2E = 1.4426950408889634

F32 = jnp.float32
BF16 = jnp.bfloat16

VMEM = pl.BlockSpec(memory_space=pltpu.VMEM)
SMEM = pl.BlockSpec(memory_space=pltpu.SMEM)
NT = (((1,), (1,)), ((), ()))


def dot(a, b):
    return jnp.dot(a, b, preferred_element_type=F32)


def dot_nt(a, b):
    return lax.dot_general(a, b, NT, preferred_element_type=F32)


def call(kernel, outs, args, smem=(), scratch=(), limit=24, work=0):
    many = isinstance(outs, list)
    kept = [
        a if i in smem else pltpu.with_memory_space_constraint(a, pltpu.VMEM) for i, a in enumerate(args)
    ]
    return pl.pallas_call(
        kernel,
        out_shape=outs,
        in_specs=[SMEM if i in smem else VMEM for i in range(len(args))],
        out_specs=[VMEM] * len(outs) if many else VMEM,
        scratch_shapes=list(scratch),
        compiler_params=pltpu.CompilerParams(vmem_limit_bytes=limit << 20),
        cost_estimate=pl.CostEstimate(flops=work, transcendentals=0, bytes_accessed=work // 100),
    )(*kept)


def counts_of(index_rows, targets):
    many = index_rows.shape[1]
    local = lax.rem(index_rows, jnp.int32(targets))
    positions = lax.broadcasted_iota(jnp.int32, (targets, many), 0)
    counts = (local[0:1, :] == positions).astype(F32)
    for row in range(1, index_rows.shape[0]):
        counts = counts + (local[row : row + 1, :] == positions).astype(F32)
    return counts


def pool_kernel(enc_ref, grid_ref, pooled_ref):
    counts = counts_of(enc_ref[...], grid_ref.shape[1]).astype(BF16)
    pooled_ref[...] = dot(grid_ref[...], counts) * (1.0 / K_ENC)


def states_of(pooled, w_in):
    values = pooled.T
    high = values.astype(BF16)
    rest = values - high.astype(F32)
    mid = rest.astype(BF16)
    low = (rest - mid.astype(F32)).astype(BF16)
    return dot(high, w_in) + (dot(mid, w_in) + dot(low, w_in))


def normed_of(states):
    centre = states - jnp.mean(states, axis=-1, keepdims=True)
    spread = jnp.mean(centre * centre, axis=-1, keepdims=True)
    return centre / jnp.sqrt(spread + EPSILON)


def own_kernel(
    pooled_ref,
    w_in_ref,
    noise_ref,
    w_gamma_ref,
    w_beta_ref,
    w_qkv_ref,
    dec_ref,
    states_ref,
    gain_ref,
    shift_ref,
    project_ref,
    counts_ref,
    inputs_ref,
):
    tok, d = states_ref.shape
    members = noise_ref.shape[0]
    gain = 1.0 + jnp.dot(noise_ref[...], w_gamma_ref[...], precision=lax.Precision.HIGHEST)
    shift = jnp.dot(noise_ref[...], w_beta_ref[...], precision=lax.Precision.HIGHEST)
    gain_ref[...] = gain
    shift_ref[...] = shift
    states = states_of(pooled_ref[...], w_in_ref[...])
    states_ref[...] = states
    normed = normed_of(states)
    for m in range(members):
        inputs_ref[m * tok : (m + 1) * tok, :] = (normed * gain[m : m + 1] + shift[m : m + 1]).astype(BF16)
    for c in range(3):
        part = dot(inputs_ref[...], w_qkv_ref[:, c * d : (c + 1) * d])
        project_ref[:, c * d : (c + 1) * d] = part.astype(BF16)
    counts = counts_of(dec_ref[...], tok).T.astype(BF16)
    counts_ref[:, :tok] = counts
    counts_ref[:, tok:] = counts


def members_kernel(
    begin,
    nbr_ref,
    pair_ref,
    next_ref,
    w_in_ref,
    gain_ref,
    shift_ref,
    project_ref,
    states_ref,
    counts_ref,
    grid_ref,
    w_qkv_ref,
    w_o_ref,
    readout_ref,
    x_ref,
    feat_ref,
    *refs,
):
    edge_ref, kv_ref, att_ref, upd_ref = refs[-4:]
    tok, d = states_ref.shape
    members = x_ref.shape[0]
    wins = tok // WIN
    wide = GROUP * HD
    windows = wins * lax.axis_size("space")
    first = lax.axis_index("space") * wins
    odd = lax.rem(lax.axis_index("space"), 2) == 1
    for slot in range(2):
        if begin == 0:
            pooled = jnp.where(odd == (slot == 0), pair_ref[...], next_ref[...])
            normed = normed_of(states_of(pooled, w_in_ref[...]))
            refs[0][slot * tok : (slot + 1) * tok, :] = normed
        else:
            normed = pair_ref[slot * tok : (slot + 1) * tok, :]
        for m in range(members):
            row = (2 * m + slot) * tok
            k = begin + m
            edge_ref[row : row + tok, :] = (
                normed * gain_ref[k : k + 1, :] + shift_ref[k : k + 1, :]
            ).astype(BF16)
    for c in range(2):
        lo = c * d
        part = dot(edge_ref[...], w_qkv_ref[:, d + lo : d + lo + d]).astype(BF16)
        for m in range(members):
            kv_ref[m, :tok, lo : lo + d] = part[2 * m * tok : (2 * m + 1) * tok]
            kv_ref[m, tok : 2 * tok, lo : lo + d] = project_ref[
                (begin + m) * tok : (begin + m + 1) * tok, d + lo : d + lo + d
            ]
            kv_ref[m, 2 * tok :, lo : lo + d] = part[(2 * m + 1) * tok : (2 * m + 2) * tok]
    head_of = lax.broadcasted_iota(jnp.int32, (WIN, wide), 1) // HD

    def attend(m, carry):
        for w in range(wins):
            starts = [(wins + w) * WIN]
            for j in range(nbr_ref.shape[1]):
                reach = lax.rem(nbr_ref[w, j] - first - w + 2 + windows, windows) + w
                starts.append(pl.multiple_of(reach * WIN, WIN))
            row = pl.multiple_of(m * tok + w * WIN, WIN)
            for g in range(HEADS // GROUP):
                lo = g * wide
                q = project_ref[pl.ds(begin * tok + row, WIN), lo : lo + wide]
                zero = jnp.zeros_like(q)
                spread = jnp.concatenate([jnp.where(head_of == h, q, zero) for h in range(GROUP)], axis=0)
                keys = jnp.concatenate([kv_ref[m, pl.ds(s, WIN), lo : lo + wide] for s in starts], axis=0)
                values = jnp.concatenate(
                    [kv_ref[m, pl.ds(s, WIN), d + lo : d + lo + wide] for s in starts], axis=0
                )
                scores = dot_nt(spread, keys) * (HD ** (-0.5) * LOG2E)
                top = jnp.max(scores, axis=-1, keepdims=True)
                weights = jnp.exp2(scores - top)
                weights = weights * (1.0 / jnp.sum(weights, axis=-1, keepdims=True))
                mixed = dot(weights.astype(BF16), values)
                out = mixed[:WIN]
                for h in range(1, GROUP):
                    out = jnp.where(head_of == h, mixed[h * WIN : (h + 1) * WIN], out)
                att_ref[pl.ds(row, WIN), lo : lo + wide] = out.astype(BF16)
        return carry

    lax.fori_loop(0, members, attend, 0)
    mixed = dot(att_ref[...], w_o_ref[...])
    for m in range(members):
        updated = states_ref[...] + mixed[m * tok : (m + 1) * tok]
        high = updated.astype(BF16)
        upd_ref[m, :tok, :] = high
        upd_ref[m, tok:, :] = (updated - high.astype(F32)).astype(BF16)

    def decode(m, carry):
        features = (dot(counts_ref[...], upd_ref[m]) / K_DEC).astype(BF16)
        feat_ref[m] = features
        x_ref[m] = (grid_ref[...].astype(F32) + dot_nt(readout_ref[...], features)).astype(BF16)
        return carry

    lax.fori_loop(0, members, decode, 0)


def pair_list(own, other):
    pairs = [(i, j) for i in range(own) for j in range(i + 1, own)]
    cross = [(i, own + j) for i in range(own) for j in range(other)]
    return pairs, cross


def stats_kernel(members, target_ref, *refs):
    out_ref = refs[-1]
    xs = [r[i].astype(F32) for r in refs[:-1] for i in range(r.shape[0])]
    truth = target_ref[...].astype(F32)
    pairs, cross = pair_list(members, len(xs) - members)
    rows = []

    def lane_sums(diff):
        col = jnp.sum(diff * diff, axis=0, keepdims=True)
        total = col[:, :LANES]
        for c in range(1, col.shape[1] // LANES):
            total = total + col[:, c * LANES : (c + 1) * LANES]
        return total

    for i in range(members):
        rows.append(lane_sums(xs[i] - truth))
    for i, j in pairs + cross:
        rows.append(lane_sums(xs[i] - xs[j]))
    row_id = lax.broadcasted_iota(jnp.int32, (32, LANES), 0)
    lane_id = lax.broadcasted_iota(jnp.int32, (32, LANES), 1)
    table = jnp.zeros((32, LANES), F32)
    for k, row in enumerate(rows):
        table = jnp.where(row_id == k, row, table)
    sums = jnp.sum(table, axis=1, keepdims=True)
    line = jnp.sum(jnp.where(row_id == lane_id, sums, 0.0), axis=0, keepdims=True)
    out_ref[...] = jnp.broadcast_to(line[None], out_ref.shape)


def slope_kernel(
    members, members_all, stat_ref, target_ref, *refs
):
    parts = (len(refs) - 4) // 3
    pred_ref, grad_ref, score_ref, pack_ref = refs[-4:]
    xs = [r[i] for r in refs[: 2 * parts] for i in range(r.shape[0])]
    feats = [r.at[i] for r in refs[2 * parts : 3 * parts] for i in range(r.shape[0])]
    xf = [x.astype(F32) for x in xs]
    truth = target_ref[...].astype(F32)
    pairs, cross = pair_list(members, members)
    total = jnp.sum(stat_ref[...].reshape(stat_ref.shape[0], LANES), axis=0, keepdims=True)
    dist = jnp.sqrt(total + EPSILON)
    lane = lax.broadcasted_iota(jnp.int32, (1, LANES), 1)
    first_cross = members + len(pairs)
    end = first_cross + len(cross)
    m = float(members_all)
    share = jnp.where(
        lane < members,
        1.0 / m,
        jnp.where(lane < first_cross, -1.0 / (m * m), jnp.where(lane < end, -0.5 / (m * m), 0.0)),
    )
    score = jnp.sum(dist * share, axis=1, keepdims=True)
    score_ref[...] = jnp.broadcast_to(score, score_ref.shape)
    pull = 1.0 / (jnp.where(lane < members, m, m * m) * dist)
    coef = {}
    for k, (i, j) in enumerate(pairs + cross):
        value = pull[:, members + k : members + k + 1]
        coef[i, j] = value
        coef[j, i] = value
    acc = None
    for i in range(members):
        pred_ref[i] = xs[i]
        slope = pull[:, i : i + 1] * (xf[i] - truth)
        for j in range(2 * members):
            if j != i:
                slope = slope + coef[i, j] * (xf[j] - xf[i])
        part = dot(slope.astype(BF16), feats[i][...])
        acc = part if acc is None else acc + part
    v, d = acc.shape
    pack_ref[...] = jnp.zeros_like(pack_ref)
    for c in range(d // LANES):
        pack_ref[c * v : (c + 1) * v, :] = acc[:, c * LANES : (c + 1) * LANES]
    grad_ref[...] = pack_ref[...].astype(BF16).reshape(grad_ref.shape)


def share_kernel(recv_ref, score_ref, out_ref):
    total = jnp.sum(recv_ref[...].astype(F32), axis=0)
    both = jnp.concatenate([total, score_ref[...]], axis=0)
    out_ref[...] = jnp.broadcast_to(both[None], out_ref.shape)


def spread_kernel(scale, recv_ref, out_ref, score_ref):
    rows = out_ref.shape[1]
    total = jnp.sum(recv_ref[...], axis=0)
    out_ref[...] = jnp.broadcast_to(total[:rows][None], out_ref.shape)
    score_ref[...] = total[rows:] * scale


def final_kernel(recv_ref, out_ref, pack_ref):
    v, d = out_ref.shape
    pack_ref[...] = recv_ref[...].reshape(pack_ref.shape)
    grad = pack_ref[...]
    square = jnp.sum(jnp.sum(grad * grad, axis=0, keepdims=True), axis=1, keepdims=True)
    scale = 1.0 / jnp.sqrt(square / (v * d) + EPSILON)
    for c in range(d // LANES):
        out_ref[:, c * LANES : (c + 1) * LANES] = pack_ref[c * v : (c + 1) * v, :] * scale


def exchange(blocks, axis):
    return lax.all_to_all(blocks, axis, split_axis=0, concat_axis=0, tiled=True)


def step(
    grid_in,
    target,
    noise,
    neighbours,
    enc_index,
    dec_index,
    w_in,
    w_gamma,
    w_beta,
    w_qkv,
    w_o,
    readout_matrix,
):
    tok = enc_index.shape[0]
    points = dec_index.shape[0]
    d = w_o.shape[0]
    members = noise.shape[1]
    v = grid_in.shape[1]
    space = lax.axis_size("space")
    grid = grid_in[0]
    truth = target[0]

    pooled = call(pool_kernel, pltpu.VMEM((v, tok), F32), (enc_index.T, grid), work=4 * 10**9)
    pairs = [(i, i ^ 1) for i in range(space)]
    nexts = [(i, (i + 1 if i % 2 else i - 1) % space) for i in range(space)]
    from_pair = lax.ppermute(pooled, "space", pairs)
    from_next = lax.ppermute(pooled, "space", nexts)
    states, gain, shift, project, counts = call(
        own_kernel,
        [
            pltpu.VMEM((tok, d), F32),
            pltpu.VMEM((members, d), F32),
            pltpu.VMEM((members, d), F32),
            pltpu.VMEM((members * tok, 3 * d), BF16),
            pltpu.VMEM((points, 2 * tok), BF16),
        ],
        (pooled, w_in, noise[0], w_gamma, w_beta, w_qkv, dec_index.T),
        scratch=(pltpu.VMEM((members * tok, d), BF16),),
        work=4 * 10**9,
    )
    own, other, feats = [], [], []
    halo = (from_pair, from_next)
    some = members // 2
    for begin in range(0, members, some):
        outs = [pltpu.VMEM((some, v, points), BF16), pltpu.VMEM((some, points, d), BF16)]
        if begin == 0:
            outs.append(pltpu.VMEM((2 * tok, d), F32))
        got = call(
            functools.partial(members_kernel, begin),
            outs,
            (
                neighbours,
                *halo,
                w_in,
                gain,
                shift,
                project,
                states,
                counts,
                grid,
                w_qkv,
                w_o,
                readout_matrix,
            ),
            smem=(0,),
            scratch=(
                pltpu.VMEM((2 * some * tok, d), BF16),
                pltpu.VMEM((some, 3 * tok, 2 * d), BF16),
                pltpu.VMEM((some * tok, d), BF16),
                pltpu.VMEM((some, 2 * tok, d), BF16),
            ),
            work=8 * 10**9,
        )
        if begin == 0:
            halo = (got[2], from_next)
        own.append(got[0])
        feats.append(got[1])
        other.append(lax.ppermute(got[0], "member", [(0, 1), (1, 0)]))
    members_all = members * lax.axis_size("member")
    stats = call(
        functools.partial(stats_kernel, members),
        pltpu.VMEM((space, 1, LANES), F32),
        (truth, *own, *other),
        work=10**9,
    )
    stats = exchange(stats, "space")
    rows = -(-v * d // (LANES * space * 8)) * 8
    pred, grad, score = call(
        functools.partial(slope_kernel, members, members_all),
        [
            jax.ShapeDtypeStruct((members, v, points), BF16),
            pltpu.VMEM((space, rows, LANES), BF16),
            pltpu.VMEM((8, LANES), F32),
        ],
        (stats, truth, *own, *other, *feats),
        scratch=(pltpu.VMEM((space * rows, LANES), F32),),
    )
    grad = exchange(grad, "space")
    peers = lax.axis_size("dp") * lax.axis_size("member")
    share = call(share_kernel, pltpu.VMEM((peers, rows + 8, LANES), F32), (grad, score))
    share = exchange(share, ("dp", "member"))
    scale = 1.0 / (lax.axis_size("dp") * (v * points * space) ** 0.5)
    spread, objective = call(
        functools.partial(spread_kernel, scale),
        [pltpu.VMEM((space, rows, LANES), F32), pltpu.VMEM((8, LANES), F32)],
        (share,),
    )
    spread = exchange(spread, "space")
    unit = call(
        final_kernel,
        jax.ShapeDtypeStruct((v, d), F32),
        (spread,),
        scratch=(pltpu.VMEM((space * rows, LANES), F32),),
    )
    return (pred[None], objective[0, 0], unit)


def solution(mesh):
    in_specs = (
        P("dp", None, "space"),
        P("dp", None, "space"),
        P("dp", "member", None),
        P("space", None),
        P("space", None),
        P("space", None),
        P(),
        P(),
        P(),
        P(),
        P(),
        P(),
    )
    out_specs = (P("dp", "member", None, "space"), P(), P())
    return jax.shard_map(step, mesh=mesh, in_specs=in_specs, out_specs=out_specs, check_vma=False)
```

```python
import functools

import jax
import jax.numpy as jnp
from jax import lax
from jax.experimental import pallas as pl
from jax.experimental.layout import Layout, with_layout_constraint
from jax.experimental.pallas import tpu as pltpu
from jax.sharding import PartitionSpec as P

HEADS = 12
HD = 64
WIN = 64
K_ENC = 4
K_DEC = 3
EPSILON = 1e-06
LANES = 128
GROUP = 4

F32 = jnp.float32
BF16 = jnp.bfloat16

VMEM = pl.BlockSpec(memory_space=pltpu.VMEM)
SMEM = pl.BlockSpec(memory_space=pltpu.SMEM)
HBM = pl.BlockSpec(memory_space=pl.ANY)
NT = (((1,), (1,)), ((), ()))


def dot(a, b):
    return jnp.dot(a, b, preferred_element_type=F32)


def dot_nt(a, b):
    return lax.dot_general(a, b, NT, preferred_element_type=F32)


def call(kernel, outs, args, smem=(), hbm=(), scratch=(), out_specs=None, limit=24, work=0):
    many = isinstance(outs, list)
    kept = [
        a if i in smem or i in hbm else pltpu.with_memory_space_constraint(a, pltpu.VMEM)
        for i, a in enumerate(args)
    ]
    return pl.pallas_call(
        kernel,
        out_shape=outs,
        in_specs=[SMEM if i in smem else HBM if i in hbm else VMEM for i in range(len(args))],
        out_specs=out_specs or ([VMEM] * len(outs) if many else VMEM),
        scratch_shapes=list(scratch),
        compiler_params=pltpu.CompilerParams(vmem_limit_bytes=limit << 20),
        cost_estimate=pl.CostEstimate(flops=work, transcendentals=0, bytes_accessed=work // 100),
    )(*kept)


def counts_of(index_rows, targets):
    many = index_rows.shape[1]
    local = lax.rem(index_rows, jnp.int32(targets))
    positions = lax.broadcasted_iota(jnp.int32, (targets, many), 0)
    counts = (local[0:1, :] == positions).astype(F32)
    for row in range(1, index_rows.shape[0]):
        counts = counts + (local[row : row + 1, :] == positions).astype(F32)
    return counts


def pool_kernel(enc_hbm, grid_hbm, pooled_ref, enc_ref, grid_ref, sems):
    copies = [
        pltpu.make_async_copy(enc_hbm, enc_ref, sems.at[0]),
        pltpu.make_async_copy(grid_hbm, grid_ref, sems.at[1]),
    ]
    for copy in copies:
        copy.start()
    copies[0].wait()
    counts = counts_of(enc_ref[...], grid_ref.shape[1]).astype(BF16)
    copies[1].wait()
    pooled_ref[...] = dot(grid_ref[...], counts) * (1.0 / K_ENC)


def states_of(pooled, w_in):
    values = pooled.T
    high = values.astype(BF16)
    rest = values - high.astype(F32)
    mid = rest.astype(BF16)
    low = (rest - mid.astype(F32)).astype(BF16)
    return dot(high, w_in) + (dot(mid, w_in) + dot(low, w_in))


def normed_of(states):
    centre = states - jnp.mean(states, axis=-1, keepdims=True)
    spread = jnp.mean(centre * centre, axis=-1, keepdims=True)
    return centre / jnp.sqrt(spread + EPSILON)


def own_kernel(
    pooled_ref,
    w_in_ref,
    noise_ref,
    w_gamma_ref,
    w_beta_ref,
    w_qkv_ref,
    dec_ref,
    states_ref,
    gain_ref,
    shift_ref,
    project_ref,
    counts_ref,
    inputs_ref,
):
    tok, d = states_ref.shape
    members = noise_ref.shape[0]
    gain = 1.0 + jnp.dot(noise_ref[...], w_gamma_ref[...], precision=lax.Precision.HIGHEST)
    shift = jnp.dot(noise_ref[...], w_beta_ref[...], precision=lax.Precision.HIGHEST)
    gain_ref[...] = gain
    shift_ref[...] = shift
    states = states_of(pooled_ref[...], w_in_ref[...])
    states_ref[...] = states
    normed = normed_of(states)
    for m in range(members):
        inputs_ref[m * tok : (m + 1) * tok, :] = (normed * gain[m : m + 1] + shift[m : m + 1]).astype(BF16)
    for c in range(3):
        part = dot(inputs_ref[...], w_qkv_ref[:, c * d : (c + 1) * d])
        if c == 0:
            part = part * HD ** (-0.5)
        project_ref[:, c * d : (c + 1) * d] = part.astype(BF16)
    counts = counts_of(dec_ref[...], tok).T.astype(BF16)
    counts_ref[:, :tok] = counts
    counts_ref[:, tok:] = counts


def members_kernel(
    begin,
    nbr_ref,
    pair_ref,
    next_ref,
    w_in_ref,
    gain_ref,
    shift_ref,
    project_ref,
    states_ref,
    counts_ref,
    grid_ref,
    w_qkv_ref,
    w_o_ref,
    readout_ref,
    x_ref,
    feat_ref,
    *refs,
):
    edge_ref, kv_ref, att_ref, upd_ref = refs[-4:]
    tok, d = states_ref.shape
    members = x_ref.shape[0]
    wins = tok // WIN
    wide = GROUP * HD
    windows = wins * lax.axis_size("space")
    first = lax.axis_index("space") * wins
    odd = lax.rem(lax.axis_index("space"), 2) == 1
    for slot in range(2):
        if begin == 0:
            pooled = jnp.where(odd == (slot == 0), pair_ref[...], next_ref[...])
            normed = normed_of(states_of(pooled, w_in_ref[...]))
            refs[0][slot * tok : (slot + 1) * tok, :] = normed
        else:
            normed = pair_ref[slot * tok : (slot + 1) * tok, :]
        for m in range(members):
            row = (2 * m + slot) * tok
            k = begin + m
            edge_ref[row : row + tok, :] = (
                normed * gain_ref[k : k + 1, :] + shift_ref[k : k + 1, :]
            ).astype(BF16)
    for c in range(2):
        lo = c * d
        part = dot(edge_ref[...], w_qkv_ref[:, d + lo : d + lo + d]).astype(BF16)
        for m in range(members):
            kv_ref[m, :tok, lo : lo + d] = part[2 * m * tok : (2 * m + 1) * tok]
            kv_ref[m, tok : 2 * tok, lo : lo + d] = project_ref[
                (begin + m) * tok : (begin + m + 1) * tok, d + lo : d + lo + d
            ]
            kv_ref[m, 2 * tok :, lo : lo + d] = part[(2 * m + 1) * tok : (2 * m + 2) * tok]
    head_of = lax.broadcasted_iota(jnp.int32, (WIN, wide), 1) // HD

    def attend(m):
        for w in range(wins):
            starts = [(wins + w) * WIN]
            for j in range(nbr_ref.shape[1]):
                reach = lax.rem(nbr_ref[w, j] - first - w + 2 + windows, windows) + w
                starts.append(pl.multiple_of(reach * WIN, WIN))
            row = m * tok + w * WIN
            for g in range(HEADS // GROUP):
                lo = g * wide
                q = project_ref[pl.ds(begin * tok + row, WIN), lo : lo + wide]
                zero = jnp.zeros_like(q)
                spread = jnp.concatenate([jnp.where(head_of == h, q, zero) for h in range(GROUP)], axis=0)
                keys = jnp.concatenate([kv_ref[m, pl.ds(s, WIN), lo : lo + wide] for s in starts], axis=0)
                values = jnp.concatenate(
                    [kv_ref[m, pl.ds(s, WIN), d + lo : d + lo + wide] for s in starts], axis=0
                )
                scores = dot_nt(spread, keys)
                top = jnp.max(scores, axis=-1, keepdims=True)
                weights = jnp.exp(scores - top)
                weights = weights * (1.0 / jnp.sum(weights, axis=-1, keepdims=True))
                mixed = dot(weights.astype(BF16), values)
                out = mixed[:WIN]
                for h in range(1, GROUP):
                    out = jnp.where(head_of == h, mixed[h * WIN : (h + 1) * WIN], out)
                att_ref[pl.ds(row, WIN), lo : lo + wide] = out.astype(BF16)

    for m in range(members):
        attend(m)
    mixed = dot(att_ref[...], w_o_ref[...])
    for m in range(members):
        updated = states_ref[...] + mixed[m * tok : (m + 1) * tok]
        high = updated.astype(BF16)
        upd_ref[m, :tok, :] = high
        upd_ref[m, tok:, :] = (updated - high.astype(F32)).astype(BF16)

    def decode(m, carry):
        features = (dot(counts_ref[...], upd_ref[m]) / K_DEC).astype(BF16)
        feat_ref[m] = features
        x_ref[m] = (grid_ref[...].astype(F32) + dot_nt(readout_ref[...], features)).astype(BF16)
        return carry

    lax.fori_loop(0, members, decode, 0)


def pair_list(own, other):
    pairs = [(i, j) for i in range(own) for j in range(i + 1, own)]
    cross = [(i, own + j) for i in range(own) for j in range(other)]
    return pairs, cross


def stats_kernel(members, target_ref, *refs):
    out_ref = refs[-1]
    xs = [r[i].astype(F32) for r in refs[:-1] for i in range(r.shape[0])]
    truth = target_ref[...].astype(F32)
    pairs, cross = pair_list(members, len(xs) - members)
    rows = []

    def lane_sums(diff):
        col = jnp.sum(diff * diff, axis=0, keepdims=True)
        total = col[:, :LANES]
        for c in range(1, col.shape[1] // LANES):
            total = total + col[:, c * LANES : (c + 1) * LANES]
        return total

    for i in range(members):
        rows.append(lane_sums(xs[i] - truth))
    for i, j in pairs + cross:
        rows.append(lane_sums(xs[i] - xs[j]))
    row_id = lax.broadcasted_iota(jnp.int32, (32, LANES), 0)
    lane_id = lax.broadcasted_iota(jnp.int32, (32, LANES), 1)
    table = jnp.zeros((32, LANES), F32)
    for k, row in enumerate(rows):
        table = jnp.where(row_id == k, row, table)
    sums = jnp.sum(table, axis=1, keepdims=True)
    line = jnp.sum(jnp.where(row_id == lane_id, sums, 0.0), axis=0, keepdims=True)
    out_ref[...] = jnp.broadcast_to(line[None], out_ref.shape)


def slope_kernel(
    members, members_all, stat_ref, target_ref, *refs
):
    parts = (len(refs) - 3) // 3
    grad_ref, score_ref, pack_ref = refs[-3:]
    xs = [r[i] for r in refs[: 2 * parts] for i in range(r.shape[0])]
    feats = [r.at[i] for r in refs[2 * parts : 3 * parts] for i in range(r.shape[0])]
    xf = [x.astype(F32) for x in xs]
    truth = target_ref[...].astype(F32)
    pairs, cross = pair_list(members, members)
    total = jnp.sum(stat_ref[...].reshape(stat_ref.shape[0], LANES), axis=0, keepdims=True)
    dist = jnp.sqrt(total + EPSILON)
    lane = lax.broadcasted_iota(jnp.int32, (1, LANES), 1)
    first_cross = members + len(pairs)
    end = first_cross + len(cross)
    m = float(members_all)
    share = jnp.where(
        lane < members,
        1.0 / m,
        jnp.where(lane < first_cross, -1.0 / (m * m), jnp.where(lane < end, -0.5 / (m * m), 0.0)),
    )
    score = jnp.sum(dist * share, axis=1, keepdims=True)
    score_ref[...] = jnp.broadcast_to(score, score_ref.shape)
    pull = 1.0 / (jnp.where(lane < members, m, m * m) * dist)
    coef = {}
    for k, (i, j) in enumerate(pairs + cross):
        value = pull[:, members + k : members + k + 1]
        coef[i, j] = value
        coef[j, i] = value
    acc = None
    for i in range(members):
        slope = pull[:, i : i + 1] * (xf[i] - truth)
        for j in range(2 * members):
            if j != i:
                slope = slope + coef[i, j] * (xf[j] - xf[i])
        part = dot(slope.astype(BF16), feats[i][...])
        acc = part if acc is None else acc + part
    v, d = acc.shape
    pack_ref[...] = jnp.zeros_like(pack_ref)
    for c in range(d // LANES):
        pack_ref[c * v : (c + 1) * v, :] = acc[:, c * LANES : (c + 1) * LANES]
    grad_ref[...] = pack_ref[...].astype(BF16).reshape(grad_ref.shape)


def share_kernel(recv_ref, score_ref, out_ref):
    total = jnp.sum(recv_ref[...].astype(F32), axis=0)
    both = jnp.concatenate([total, score_ref[...]], axis=0)
    out_ref[...] = jnp.broadcast_to(both[None], out_ref.shape)


def spread_kernel(recv_ref, out_ref, score_ref):
    rows = out_ref.shape[1]
    total = jnp.sum(recv_ref[...], axis=0)
    out_ref[...] = jnp.broadcast_to(total[:rows][None], out_ref.shape)
    score_ref[...] = total[rows:]


def final_kernel(scale, recv_ref, score_ref, out_ref, objective_ref, pack_ref):
    v, d = out_ref.shape
    objective_ref[0] = jnp.max(score_ref[...]) * scale
    pack_ref[...] = recv_ref[...].reshape(pack_ref.shape)
    grad = pack_ref[...]
    square = jnp.sum(jnp.sum(grad * grad, axis=0, keepdims=True), axis=1, keepdims=True)
    scale = 1.0 / jnp.sqrt(square / (v * d) + EPSILON)
    for c in range(d // LANES):
        out_ref[:, c * LANES : (c + 1) * LANES] = pack_ref[c * v : (c + 1) * v, :] * scale


def exchange(blocks, axis):
    return lax.all_to_all(blocks, axis, split_axis=0, concat_axis=0, tiled=True)


def step(
    grid_in,
    target,
    noise,
    neighbours,
    enc_index,
    dec_index,
    w_in,
    w_gamma,
    w_beta,
    w_qkv,
    w_o,
    readout_matrix,
):
    tok = enc_index.shape[0]
    points = dec_index.shape[0]
    d = w_o.shape[0]
    members = noise.shape[1]
    v = grid_in.shape[1]
    space = lax.axis_size("space")
    grid = grid_in[0]
    truth = target[0]

    pooled = call(
        pool_kernel,
        pltpu.VMEM((v, tok), F32),
        (enc_index.T, grid),
        hbm=(0, 1),
        scratch=(
            pltpu.VMEM((enc_index.shape[1], tok), jnp.int32),
            pltpu.VMEM((v, points), BF16),
            pltpu.SemaphoreType.DMA((2,)),
        ),
        work=4 * 10**9,
    )
    pairs = [(i, i ^ 1) for i in range(space)]
    nexts = [(i, (i + 1 if i % 2 else i - 1) % space) for i in range(space)]
    from_pair = lax.ppermute(pooled, "space", pairs)
    from_next = lax.ppermute(pooled, "space", nexts)
    states, gain, shift, project, counts = call(
        own_kernel,
        [
            pltpu.VMEM((tok, d), F32),
            pltpu.VMEM((members, d), F32),
            pltpu.VMEM((members, d), F32),
            pltpu.VMEM((members * tok, 3 * d), BF16),
            pltpu.VMEM((points, 2 * tok), BF16),
        ],
        (pooled, w_in, noise[0], w_gamma, w_beta, w_qkv, dec_index.T),
        scratch=(pltpu.VMEM((members * tok, d), BF16),),
        work=4 * 10**9,
    )
    own, other, feats = [], [], []
    halo = (from_pair, from_next)
    some = members // 2
    for begin in range(0, members, some):
        outs = [pltpu.VMEM((some, v, points), BF16), pltpu.VMEM((some, points, d), BF16)]
        if begin == 0:
            outs.append(pltpu.VMEM((2 * tok, d), F32))
        got = call(
            functools.partial(members_kernel, begin),
            outs,
            (
                neighbours,
                *halo,
                w_in,
                gain,
                shift,
                project,
                states,
                counts,
                grid,
                w_qkv,
                w_o,
                readout_matrix,
            ),
            smem=(0,),
            scratch=(
                pltpu.VMEM((2 * some * tok, d), BF16),
                pltpu.VMEM((some, 3 * tok, 2 * d), BF16),
                pltpu.VMEM((some * tok, d), BF16),
                pltpu.VMEM((some, 2 * tok, d), BF16),
            ),
            work=8 * 10**9,
        )
        if begin == 0:
            halo = (got[2], from_next)
        own.append(got[0])
        feats.append(got[1])
        other.append(lax.ppermute(got[0], "member", [(0, 1), (1, 0)]))
    pred = jnp.concatenate([x.transpose(1, 0, 2) for x in own], axis=1)
    pred = with_layout_constraint(pred, Layout(major_to_minor=(0, 1, 2)))
    pred, other[-1] = lax.optimization_barrier((pred, other[-1]))
    pred = pred.transpose(1, 0, 2)
    members_all = members * lax.axis_size("member")
    stats = call(
        functools.partial(stats_kernel, members),
        pltpu.VMEM((space, 1, LANES), F32),
        (truth, *own, *other),
        work=10**9,
    )
    stats = exchange(stats, "space")
    rows = -(-v * d // (LANES * space * 8)) * 8
    grad, score = call(
        functools.partial(slope_kernel, members, members_all),
        [
            pltpu.VMEM((space, rows, LANES), BF16),
            pltpu.VMEM((8, LANES), F32),
        ],
        (stats, truth, *own, *other, *feats),
        scratch=(pltpu.VMEM((space * rows, LANES), F32),),
    )
    grad = exchange(grad, "space")
    peers = lax.axis_size("dp") * lax.axis_size("member")
    share = call(share_kernel, pltpu.VMEM((peers, rows + 8, LANES), F32), (grad, score))
    share = exchange(share, ("dp", "member"))
    scale = 1.0 / (lax.axis_size("dp") * (v * points * space) ** 0.5)
    spread, score = call(
        spread_kernel,
        [pltpu.VMEM((space, rows, LANES), F32), pltpu.VMEM((8, LANES), F32)],
        (share,),
    )
    spread = exchange(spread, "space")
    unit, objective = call(
        functools.partial(final_kernel, scale),
        [jax.ShapeDtypeStruct((v, d), F32), jax.ShapeDtypeStruct((1,), F32)],
        (spread, score),
        out_specs=[VMEM, SMEM],
        scratch=(pltpu.VMEM((space * rows, LANES), F32),),
    )
    return (pred[None], objective.reshape(()), unit)


def solution(mesh):
    in_specs = (
        P("dp", None, "space"),
        P("dp", None, "space"),
        P("dp", "member", None),
        P("space", None),
        P("space", None),
        P("space", None),
        P(),
        P(),
        P(),
        P(),
        P(),
        P(),
    )
    out_specs = (P("dp", "member", None, "space"), P(), P())
    return jax.shard_map(step, mesh=mesh, in_specs=in_specs, out_specs=out_specs, check_vma=False)
```

```python
import functools

import jax
import jax.numpy as jnp
from jax import lax
from jax.experimental import pallas as pl
from jax.experimental.layout import Layout, with_layout_constraint
from jax.experimental.pallas import tpu as pltpu
from jax.sharding import PartitionSpec as P

HEADS = 12
HD = 64
WIN = 64
K_ENC = 4
K_DEC = 3
EPSILON = 1e-06
LANES = 128
GROUP = 4
CHUNKS = (2, 1, 1)

F32 = jnp.float32
BF16 = jnp.bfloat16

VMEM = pl.BlockSpec(memory_space=pltpu.VMEM)
SMEM = pl.BlockSpec(memory_space=pltpu.SMEM)
HBM = pl.BlockSpec(memory_space=pltpu.HBM)
NT = (((1,), (1,)), ((), ()))


def dot(a, b):
    return jnp.dot(a, b, preferred_element_type=F32)


def dot_nt(a, b):
    return lax.dot_general(a, b, NT, preferred_element_type=F32)


def call(kernel, outs, args, smem=(), hbm=(), scratch=(), out_specs=None, limit=24, work=0):
    many = isinstance(outs, list)
    kept = [
        a if i in smem else pltpu.with_memory_space_constraint(a, pltpu.HBM if i in hbm else pltpu.VMEM)
        for i, a in enumerate(args)
    ]
    return pl.pallas_call(
        kernel,
        out_shape=outs,
        in_specs=[SMEM if i in smem else HBM if i in hbm else VMEM for i in range(len(args))],
        out_specs=out_specs or ([VMEM] * len(outs) if many else VMEM),
        scratch_shapes=list(scratch),
        compiler_params=pltpu.CompilerParams(vmem_limit_bytes=limit << 20),
        cost_estimate=pl.CostEstimate(flops=work, transcendentals=0, bytes_accessed=work // 100),
    )(*kept)


def counts_of(index_rows, targets):
    many = index_rows.shape[1]
    local = lax.rem(index_rows, jnp.int32(targets))
    positions = lax.broadcasted_iota(jnp.int32, (targets, many), 0)
    counts = (local[0:1, :] == positions).astype(F32)
    for row in range(1, index_rows.shape[0]):
        counts = counts + (local[row : row + 1, :] == positions).astype(F32)
    return counts


def pool_kernel(enc_hbm, grid_hbm, pooled_ref, enc_ref, grid_ref, sems):
    copies = [
        pltpu.make_async_copy(enc_hbm, enc_ref, sems.at[0]),
        pltpu.make_async_copy(grid_hbm, grid_ref, sems.at[1]),
    ]
    for copy in copies:
        copy.start()
    copies[0].wait()
    counts = counts_of(enc_ref[...], grid_ref.shape[1]).astype(BF16)
    copies[1].wait()
    pooled_ref[...] = dot(grid_ref[...], counts) * (1.0 / K_ENC)


def states_of(pooled, w_in):
    values = pooled.T
    high = values.astype(BF16)
    rest = values - high.astype(F32)
    mid = rest.astype(BF16)
    low = (rest - mid.astype(F32)).astype(BF16)
    return dot(high, w_in) + (dot(mid, w_in) + dot(low, w_in))


def normed_of(states):
    centre = states - jnp.mean(states, axis=-1, keepdims=True)
    spread = jnp.mean(centre * centre, axis=-1, keepdims=True)
    return centre / jnp.sqrt(spread + EPSILON)


def own_kernel(
    pooled_ref,
    w_in_ref,
    noise_ref,
    w_gamma_ref,
    w_beta_ref,
    w_qkv_ref,
    dec_ref,
    states_ref,
    gain_ref,
    shift_ref,
    project_ref,
    counts_ref,
    inputs_ref,
):
    tok, d = states_ref.shape
    members = noise_ref.shape[0]
    gain = 1.0 + jnp.dot(noise_ref[...], w_gamma_ref[...], precision=lax.Precision.HIGHEST)
    shift = jnp.dot(noise_ref[...], w_beta_ref[...], precision=lax.Precision.HIGHEST)
    gain_ref[...] = gain
    shift_ref[...] = shift
    states = states_of(pooled_ref[...], w_in_ref[...])
    states_ref[...] = states
    normed = normed_of(states)
    for m in range(members):
        inputs_ref[m * tok : (m + 1) * tok, :] = (normed * gain[m : m + 1] + shift[m : m + 1]).astype(BF16)
    for c in range(3):
        part = dot(inputs_ref[...], w_qkv_ref[:, c * d : (c + 1) * d])
        if c == 0:
            part = part * HD ** (-0.5)
        project_ref[:, c * d : (c + 1) * d] = part.astype(BF16)
    counts = counts_of(dec_ref[...], tok).T.astype(BF16)
    counts_ref[:, :tok] = counts
    counts_ref[:, tok:] = counts


def members_kernel(
    begin,
    nbr_ref,
    pair_ref,
    next_ref,
    w_in_ref,
    gain_ref,
    shift_ref,
    project_ref,
    states_ref,
    counts_ref,
    grid_ref,
    w_qkv_ref,
    w_o_ref,
    readout_ref,
    x_ref,
    feat_ref,
    *refs,
):
    edge_ref, kv_ref, att_ref, upd_ref = refs[-4:]
    tok, d = states_ref.shape
    members = x_ref.shape[0]
    wins = tok // WIN
    wide = GROUP * HD
    windows = wins * lax.axis_size("space")
    first = lax.axis_index("space") * wins
    odd = lax.rem(lax.axis_index("space"), 2) == 1
    for slot in range(2):
        if begin == 0:
            pooled = jnp.where(odd == (slot == 0), pair_ref[...], next_ref[...])
            normed = normed_of(states_of(pooled, w_in_ref[...]))
            refs[0][slot * tok : (slot + 1) * tok, :] = normed
        else:
            normed = pair_ref[slot * tok : (slot + 1) * tok, :]
        for m in range(members):
            row = (2 * m + slot) * tok
            k = begin + m
            edge_ref[row : row + tok, :] = (
                normed * gain_ref[k : k + 1, :] + shift_ref[k : k + 1, :]
            ).astype(BF16)
    for c in range(2):
        lo = c * d
        part = dot(edge_ref[...], w_qkv_ref[:, d + lo : d + lo + d]).astype(BF16)
        for m in range(members):
            kv_ref[m, :tok, lo : lo + d] = part[2 * m * tok : (2 * m + 1) * tok]
            kv_ref[m, tok : 2 * tok, lo : lo + d] = project_ref[
                (begin + m) * tok : (begin + m + 1) * tok, d + lo : d + lo + d
            ]
            kv_ref[m, 2 * tok :, lo : lo + d] = part[(2 * m + 1) * tok : (2 * m + 2) * tok]
    head_of = lax.broadcasted_iota(jnp.int32, (WIN, wide), 1) // HD

    def attend(m):
        for w in range(wins):
            starts = [(wins + w) * WIN]
            for j in range(nbr_ref.shape[1]):
                reach = lax.rem(nbr_ref[w, j] - first - w + 2 + windows, windows) + w
                starts.append(pl.multiple_of(reach * WIN, WIN))
            row = m * tok + w * WIN
            for g in range(HEADS // GROUP):
                lo = g * wide
                q = project_ref[pl.ds(begin * tok + row, WIN), lo : lo + wide]
                zero = jnp.zeros_like(q)
                spread = jnp.concatenate([jnp.where(head_of == h, q, zero) for h in range(GROUP)], axis=0)
                keys = jnp.concatenate([kv_ref[m, pl.ds(s, WIN), lo : lo + wide] for s in starts], axis=0)
                values = jnp.concatenate(
                    [kv_ref[m, pl.ds(s, WIN), d + lo : d + lo + wide] for s in starts], axis=0
                )
                scores = dot_nt(spread, keys)
                top = jnp.max(scores, axis=-1, keepdims=True)
                weights = jnp.exp(scores - top)
                weights = weights * (1.0 / jnp.sum(weights, axis=-1, keepdims=True))
                mixed = dot(weights.astype(BF16), values)
                out = mixed[:WIN]
                for h in range(1, GROUP):
                    out = jnp.where(head_of == h, mixed[h * WIN : (h + 1) * WIN], out)
                att_ref[pl.ds(row, WIN), lo : lo + wide] = out.astype(BF16)

    for m in range(members):
        attend(m)
    mixed = dot(att_ref[...], w_o_ref[...])
    for m in range(members):
        updated = states_ref[...] + mixed[m * tok : (m + 1) * tok]
        high = updated.astype(BF16)
        upd_ref[m, :tok, :] = high
        upd_ref[m, tok:, :] = (updated - high.astype(F32)).astype(BF16)

    def decode(m, carry):
        features = (dot(counts_ref[...], upd_ref[m]) / K_DEC).astype(BF16)
        feat_ref[m] = features
        x_ref[m] = (grid_ref[...].astype(F32) + dot_nt(readout_ref[...], features)).astype(BF16)
        return carry

    lax.fori_loop(0, members, decode, 0)


def pair_list(own, other):
    pairs = [(i, j) for i in range(own) for j in range(i + 1, own)]
    cross = [(i, own + j) for i in range(own) for j in range(other)]
    return pairs, cross


def stats_kernel(members, target_ref, *refs):
    out_ref = refs[-1]
    xs = [r[i].astype(F32) for r in refs[:-1] for i in range(r.shape[0])]
    truth = target_ref[...].astype(F32)
    pairs, cross = pair_list(members, len(xs) - members)
    rows = []

    def lane_sums(diff):
        col = jnp.sum(diff * diff, axis=0, keepdims=True)
        total = col[:, :LANES]
        for c in range(1, col.shape[1] // LANES):
            total = total + col[:, c * LANES : (c + 1) * LANES]
        return total

    for i in range(members):
        rows.append(lane_sums(xs[i] - truth))
    for i, j in pairs + cross:
        rows.append(lane_sums(xs[i] - xs[j]))
    row_id = lax.broadcasted_iota(jnp.int32, (32, LANES), 0)
    lane_id = lax.broadcasted_iota(jnp.int32, (32, LANES), 1)
    table = jnp.zeros((32, LANES), F32)
    for k, row in enumerate(rows):
        table = jnp.where(row_id == k, row, table)
    sums = jnp.sum(table, axis=1, keepdims=True)
    line = jnp.sum(jnp.where(row_id == lane_id, sums, 0.0), axis=0, keepdims=True)
    out_ref[...] = jnp.broadcast_to(line[None], out_ref.shape)


def slope_kernel(
    members, members_all, stat_ref, target_ref, *refs
):
    parts = (len(refs) - 3) // 3
    grad_ref, score_ref, pack_ref = refs[-3:]
    xs = [r[i] for r in refs[: 2 * parts] for i in range(r.shape[0])]
    feats = [r.at[i] for r in refs[2 * parts : 3 * parts] for i in range(r.shape[0])]
    xf = [x.astype(F32) for x in xs]
    truth = target_ref[...].astype(F32)
    pairs, cross = pair_list(members, members)
    total = jnp.sum(stat_ref[...].reshape(stat_ref.shape[0], LANES), axis=0, keepdims=True)
    dist = jnp.sqrt(total + EPSILON)
    lane = lax.broadcasted_iota(jnp.int32, (1, LANES), 1)
    first_cross = members + len(pairs)
    end = first_cross + len(cross)
    m = float(members_all)
    share = jnp.where(
        lane < members,
        1.0 / m,
        jnp.where(lane < first_cross, -1.0 / (m * m), jnp.where(lane < end, -0.5 / (m * m), 0.0)),
    )
    score = jnp.sum(dist * share, axis=1, keepdims=True)
    score_ref[...] = jnp.broadcast_to(score, score_ref.shape)
    pull = 1.0 / (jnp.where(lane < members, m, m * m) * dist)
    coef = {}
    for k, (i, j) in enumerate(pairs + cross):
        value = pull[:, members + k : members + k + 1]
        coef[i, j] = value
        coef[j, i] = value
    acc = None
    for i in range(members):
        slope = pull[:, i : i + 1] * (xf[i] - truth)
        for j in range(2 * members):
            if j != i:
                slope = slope + coef[i, j] * (xf[j] - xf[i])
        part = dot(slope.astype(BF16), feats[i][...])
        acc = part if acc is None else acc + part
    v, d = acc.shape
    pack_ref[...] = jnp.zeros_like(pack_ref)
    for c in range(d // LANES):
        pack_ref[c * v : (c + 1) * v, :] = acc[:, c * LANES : (c + 1) * LANES]
    grad_ref[...] = pack_ref[...].astype(BF16).reshape(grad_ref.shape)


def share_kernel(spare, recv_ref, score_ref, out_ref):
    total = jnp.sum(recv_ref[...].astype(F32), axis=0)
    rows = lax.broadcasted_iota(jnp.int32, total.shape, 0)
    last = lax.axis_index("space") == lax.axis_size("space") - 1
    score = jnp.broadcast_to(score_ref[0:1, :], total.shape)
    total = jnp.where(jnp.logical_and(last, rows >= spare), score, total)
    out_ref[...] = jnp.broadcast_to(total[None], out_ref.shape)


def spread_kernel(spare, recv_ref, out_ref):
    total = jnp.sum(recv_ref[...], axis=0)
    rows = lax.broadcasted_iota(jnp.int32, total.shape, 0)
    last = lax.axis_index("space") == lax.axis_size("space") - 1
    high = total.astype(BF16)
    low = (total - high.astype(F32)).astype(BF16)
    sent = jnp.where(jnp.logical_and(last, rows > spare), low.astype(F32), high.astype(F32)).astype(BF16)
    out_ref[...] = jnp.broadcast_to(sent[None], out_ref.shape)


def final_kernel(scale, recv_ref, out_ref, objective_ref, pack_ref):
    v, d = out_ref.shape
    used = v * d // LANES
    pack_ref[...] = recv_ref[...].reshape(pack_ref.shape).astype(F32)
    tail = pack_ref[used : used + 8, :]
    objective_ref[0] = jnp.max(tail[0:1, :] + tail[1:2, :]) * scale
    grad = pack_ref[:used, :]
    square = jnp.sum(jnp.sum(grad * grad, axis=0, keepdims=True), axis=1, keepdims=True)
    factor = 1.0 / jnp.sqrt(square / (v * d) + EPSILON)
    for c in range(d // LANES):
        out_ref[:, c * LANES : (c + 1) * LANES] = pack_ref[c * v : (c + 1) * v, :] * factor


def exchange(blocks, axis):
    return lax.all_to_all(blocks, axis, split_axis=0, concat_axis=0, tiled=True)


def step(
    grid_in,
    target,
    noise,
    neighbours,
    enc_index,
    dec_index,
    w_in,
    w_gamma,
    w_beta,
    w_qkv,
    w_o,
    readout_matrix,
):
    tok = enc_index.shape[0]
    points = dec_index.shape[0]
    d = w_o.shape[0]
    members = noise.shape[1]
    v = grid_in.shape[1]
    space = lax.axis_size("space")
    grid = grid_in[0]
    truth = target[0]

    pooled = call(
        pool_kernel,
        pltpu.VMEM((v, tok), F32),
        (enc_index.T, grid),
        hbm=(0, 1),
        scratch=(
            pltpu.VMEM((enc_index.shape[1], tok), jnp.int32),
            pltpu.VMEM((v, points), BF16),
            pltpu.SemaphoreType.DMA((2,)),
        ),
        work=4 * 10**9,
    )
    pairs = [(i, i ^ 1) for i in range(space)]
    nexts = [(i, (i + 1 if i % 2 else i - 1) % space) for i in range(space)]
    from_pair = lax.ppermute(pooled, "space", pairs)
    from_next = lax.ppermute(pooled, "space", nexts)
    states, gain, shift, project, counts = call(
        own_kernel,
        [
            pltpu.VMEM((tok, d), F32),
            pltpu.VMEM((members, d), F32),
            pltpu.VMEM((members, d), F32),
            pltpu.VMEM((members * tok, 3 * d), BF16),
            pltpu.VMEM((points, 2 * tok), BF16),
        ],
        (pooled, w_in, noise[0], w_gamma, w_beta, w_qkv, dec_index.T),
        scratch=(pltpu.VMEM((members * tok, d), BF16),),
        work=4 * 10**9,
    )
    own, other, feats = [], [], []
    halo = (from_pair, from_next)
    begin = 0
    for some in CHUNKS:
        outs = [pltpu.VMEM((some, v, points), BF16), pltpu.VMEM((some, points, d), BF16)]
        if begin == 0:
            outs.append(pltpu.VMEM((2 * tok, d), F32))
        got = call(
            functools.partial(members_kernel, begin),
            outs,
            (
                neighbours,
                *halo,
                w_in,
                gain,
                shift,
                project,
                states,
                counts,
                grid,
                w_qkv,
                w_o,
                readout_matrix,
            ),
            smem=(0,),
            scratch=(
                pltpu.VMEM((2 * some * tok, d), BF16),
                pltpu.VMEM((some, 3 * tok, 2 * d), BF16),
                pltpu.VMEM((some * tok, d), BF16),
                pltpu.VMEM((some, 2 * tok, d), BF16),
            ),
            work=8 * 10**9,
        )
        if begin == 0:
            halo = (got[2], from_next)
        own.append(got[0])
        feats.append(got[1])
        other.append(lax.ppermute(got[0], "member", [(0, 1), (1, 0)]))
        begin += some
    pred = jnp.concatenate([x.transpose(1, 0, 2) for x in own], axis=1)
    pred = with_layout_constraint(pred, Layout(major_to_minor=(0, 1, 2)))
    pred, other[-1] = lax.optimization_barrier((pred, other[-1]))
    pred = pred.transpose(1, 0, 2)
    members_all = members * lax.axis_size("member")
    stats = call(
        functools.partial(stats_kernel, members),
        pltpu.VMEM((space, 1, LANES), F32),
        (truth, *own, *other),
        work=10**9,
    )
    stats = exchange(stats, "space")
    rows = -(-v * d // (LANES * space * 8)) * 8
    grad, score = call(
        functools.partial(slope_kernel, members, members_all),
        [
            pltpu.VMEM((space, rows, LANES), BF16),
            pltpu.VMEM((8, LANES), F32),
        ],
        (stats, truth, *own, *other, *feats),
        scratch=(pltpu.VMEM((space * rows, LANES), F32),),
    )
    grad = exchange(grad, "space")
    peers = lax.axis_size("dp") * lax.axis_size("member")
    spare = v * d // LANES - (space - 1) * rows
    assert 0 < spare <= rows - 2
    share = call(
        functools.partial(share_kernel, spare), pltpu.VMEM((peers, rows, LANES), F32), (grad, score)
    )
    share = exchange(share, ("dp", "member"))
    scale = 1.0 / (lax.axis_size("dp") * (v * points * space) ** 0.5)
    spread = call(
        functools.partial(spread_kernel, spare), pltpu.VMEM((space, rows, LANES), BF16), (share,)
    )
    spread = exchange(spread, "space")
    unit, objective = call(
        functools.partial(final_kernel, scale),
        [jax.ShapeDtypeStruct((v, d), F32), jax.ShapeDtypeStruct((1,), F32)],
        (spread,),
        out_specs=[VMEM, SMEM],
        scratch=(pltpu.VMEM((space * rows, LANES), F32),),
    )
    return (pred[None], objective.reshape(()), unit)


def solution(mesh):
    in_specs = (
        P("dp", None, "space"),
        P("dp", None, "space"),
        P("dp", "member", None),
        P("space", None),
        P("space", None),
        P("space", None),
        P(),
        P(),
        P(),
        P(),
        P(),
        P(),
    )
    out_specs = (P("dp", "member", None, "space"), P(), P())
    return jax.shard_map(step, mesh=mesh, in_specs=in_specs, out_specs=out_specs, check_vma=False)
```

```python
import functools

import jax
import jax.numpy as jnp
from jax import lax
from jax.experimental import pallas as pl
from jax.experimental.pallas import tpu as pltpu
from jax.sharding import PartitionSpec as P

HEADS = 12
HD = 64
WIN = 64
K_ENC = 4
K_DEC = 3
EPSILON = 1e-06
LANES = 128
GROUP = 4

F32 = jnp.float32
BF16 = jnp.bfloat16

VMEM = pl.BlockSpec(memory_space=pltpu.VMEM)
SMEM = pl.BlockSpec(memory_space=pltpu.SMEM)
HBM = pl.BlockSpec(memory_space=pltpu.HBM)
NT = (((1,), (1,)), ((), ()))


def dot(a, b):
    return jnp.dot(a, b, preferred_element_type=F32)


def dot_nt(a, b):
    return lax.dot_general(a, b, NT, preferred_element_type=F32)


def call(kernel, outs, args, smem=(), hbm=(), scratch=(), out_specs=None, limit=24, work=0):
    many = isinstance(outs, list)
    kept = [
        a if i in smem else pltpu.with_memory_space_constraint(a, pltpu.HBM if i in hbm else pltpu.VMEM)
        for i, a in enumerate(args)
    ]
    return pl.pallas_call(
        kernel,
        out_shape=outs,
        in_specs=[SMEM if i in smem else HBM if i in hbm else VMEM for i in range(len(args))],
        out_specs=out_specs or ([VMEM] * len(outs) if many else VMEM),
        scratch_shapes=list(scratch),
        compiler_params=pltpu.CompilerParams(vmem_limit_bytes=limit << 20),
        cost_estimate=pl.CostEstimate(flops=work, transcendentals=0, bytes_accessed=work // 100),
    )(*kept)


def counts_of(index_rows, targets):
    many = index_rows.shape[1]
    local = lax.rem(index_rows, jnp.int32(targets))
    positions = lax.broadcasted_iota(jnp.int32, (targets, many), 0)
    counts = (local[0:1, :] == positions).astype(F32)
    for row in range(1, index_rows.shape[0]):
        counts = counts + (local[row : row + 1, :] == positions).astype(F32)
    return counts


def pool_kernel(enc_hbm, grid_hbm, noise_hbm, pooled_ref, enc_ref, grid_ref, noise_ref, sems):
    copies = [
        pltpu.make_async_copy(enc_hbm, enc_ref, sems.at[0]),
        pltpu.make_async_copy(grid_hbm, grid_ref, sems.at[1]),
        pltpu.make_async_copy(noise_hbm, noise_ref, sems.at[2]),
    ]
    for copy in copies:
        copy.start()
    copies[0].wait()
    counts = counts_of(enc_ref[...], grid_ref.shape[1]).astype(BF16)
    copies[1].wait()
    copies[2].wait()
    v = grid_ref.shape[0]
    pooled_ref[:v, :] = dot(grid_ref[...], counts) * (1.0 / K_ENC)
    pooled_ref[v:, :] = jnp.zeros((pooled_ref.shape[0] - v, pooled_ref.shape[1]), F32)
    members, nz = noise_ref.shape
    pooled_ref[v : v + members, :nz] = noise_ref[...]


def states_of(pooled, w_in):
    values = pooled[: w_in.shape[0]].T
    high = values.astype(BF16)
    rest = values - high.astype(F32)
    mid = rest.astype(BF16)
    low = (rest - mid.astype(F32)).astype(BF16)
    return dot(high, w_in) + (dot(mid, w_in) + dot(low, w_in))


def normed_of(states):
    centre = states - jnp.mean(states, axis=-1, keepdims=True)
    spread = jnp.mean(centre * centre, axis=-1, keepdims=True)
    return centre / jnp.sqrt(spread + EPSILON)


def conditioning(noise, w_gamma, w_beta):
    gain = 1.0 + jnp.dot(noise, w_gamma, precision=lax.Precision.HIGHEST)
    return gain, jnp.dot(noise, w_beta, precision=lax.Precision.HIGHEST)


def project_into(out_ref, inputs, w_qkv_ref):
    d = w_qkv_ref.shape[0]
    for c in range(3):
        part = dot(inputs, w_qkv_ref[:, c * d : (c + 1) * d])
        if c == 0:
            part = part * HD ** (-0.5)
        out_ref[:, c * d : (c + 1) * d] = part.astype(BF16)


def own_kernel(
    pooled_ref,
    w_in_ref,
    noise_ref,
    w_gamma_ref,
    w_beta_ref,
    w_qkv_ref,
    dec_ref,
    states_ref,
    gain_ref,
    shift_ref,
    project_ref,
    counts_ref,
    inputs_ref,
):
    tok, _ = states_ref.shape
    members = noise_ref.shape[0]
    gain, shift = conditioning(noise_ref[...], w_gamma_ref[...], w_beta_ref[...])
    gain_ref[...] = gain
    shift_ref[...] = shift
    states = states_of(pooled_ref[...], w_in_ref[...])
    states_ref[...] = states
    normed = normed_of(states)
    for m in range(members):
        inputs_ref[m * tok : (m + 1) * tok, :] = (normed * gain[m : m + 1] + shift[m : m + 1]).astype(BF16)
    project_into(project_ref, inputs_ref[...], w_qkv_ref)
    counts = counts_of(dec_ref[...], tok).T.astype(BF16)
    counts_ref[:, :tok] = counts
    counts_ref[:, tok:] = counts


def members_kernel(
    begin,
    own,
    nbr_ref,
    pair_ref,
    next_ref,
    w_in_ref,
    w_gamma_ref,
    w_beta_ref,
    gain_ref,
    shift_ref,
    project_ref,
    states_ref,
    counts_ref,
    grid_ref,
    w_qkv_ref,
    w_o_ref,
    readout_ref,
    x_ref,
    feat_ref,
    extra_ref,
    *refs,
):
    edge_ref, kv_ref, att_ref, upd_ref = refs[:4]
    tok, d = states_ref.shape
    members = kv_ref.shape[0]
    gains = [gain_ref[begin + m : begin + m + 1, :] for m in range(own)]
    shifts = [shift_ref[begin + m : begin + m + 1, :] for m in range(own)]
    sources = [(project_ref, (begin + m) * tok) for m in range(own)]
    if members > own:
        mine_ref = refs[4]
        v, count = w_in_ref.shape[0], gain_ref.shape[0]
        noise = next_ref[v : v + count, : w_gamma_ref.shape[0]]
        gain, shift = conditioning(noise, w_gamma_ref[...], w_beta_ref[...])
        normed = normed_of(states_ref[...])
        rows = []
        for m in range(members - own):
            k = begin + m
            gains.append(gain[k : k + 1])
            shifts.append(shift[k : k + 1])
            sources.append((mine_ref, m * tok))
            rows.append((normed * gains[-1] + shifts[-1]).astype(BF16))
        project_into(mine_ref, jnp.concatenate(rows, axis=0), w_qkv_ref)
    wins = tok // WIN
    wide = GROUP * HD
    windows = wins * lax.axis_size("space")
    first = lax.axis_index("space") * wins
    odd = lax.rem(lax.axis_index("space"), 2) == 1
    for slot in range(2):
        if begin == 0:
            pooled = jnp.where(odd == (slot == 0), pair_ref[...], next_ref[...])
            normed = normed_of(states_of(pooled, w_in_ref[...]))
            extra_ref[slot * tok : (slot + 1) * tok, :] = normed
        else:
            normed = pair_ref[slot * tok : (slot + 1) * tok, :]
        for m in range(members):
            row = (2 * m + slot) * tok
            edge_ref[row : row + tok, :] = (normed * gains[m] + shifts[m]).astype(BF16)
    for c in range(2):
        lo = c * d
        part = dot(edge_ref[...], w_qkv_ref[:, d + lo : d + lo + d]).astype(BF16)
        for m in range(members):
            kv_ref[m, :tok, lo : lo + d] = part[2 * m * tok : (2 * m + 1) * tok]
            ref, row = sources[m]
            kv_ref[m, tok : 2 * tok, lo : lo + d] = ref[row : row + tok, d + lo : d + lo + d]
            kv_ref[m, 2 * tok :, lo : lo + d] = part[(2 * m + 1) * tok : (2 * m + 2) * tok]
    head_of = lax.broadcasted_iota(jnp.int32, (WIN, wide), 1) // HD

    def attend(m):
        for w in range(wins):
            starts = [(wins + w) * WIN]
            for j in range(nbr_ref.shape[1]):
                reach = lax.rem(nbr_ref[w, j] - first - w + 2 + windows, windows) + w
                starts.append(pl.multiple_of(reach * WIN, WIN))
            row = m * tok + w * WIN
            for g in range(HEADS // GROUP):
                lo = g * wide
                ref, base = sources[m]
                q = ref[base + w * WIN : base + (w + 1) * WIN, lo : lo + wide]
                zero = jnp.zeros_like(q)
                spread = jnp.concatenate([jnp.where(head_of == h, q, zero) for h in range(GROUP)], axis=0)
                keys = jnp.concatenate([kv_ref[m, pl.ds(s, WIN), lo : lo + wide] for s in starts], axis=0)
                values = jnp.concatenate(
                    [kv_ref[m, pl.ds(s, WIN), d + lo : d + lo + wide] for s in starts], axis=0
                )
                scores = dot_nt(spread, keys)
                top = jnp.max(scores, axis=-1, keepdims=True)
                weights = jnp.exp(scores - top)
                weights = weights * (1.0 / jnp.sum(weights, axis=-1, keepdims=True))
                mixed = dot(weights.astype(BF16), values)
                out = mixed[:WIN]
                for h in range(1, GROUP):
                    out = jnp.where(head_of == h, mixed[h * WIN : (h + 1) * WIN], out)
                att_ref[row : row + WIN, lo : lo + wide] = out.astype(BF16)

    for m in range(members):
        attend(m)
    mixed = dot(att_ref[...], w_o_ref[...])
    for m in range(members):
        updated = states_ref[...] + mixed[m * tok : (m + 1) * tok]
        high = updated.astype(BF16)
        upd_ref[m, :tok, :] = high
        upd_ref[m, tok:, :] = (updated - high.astype(F32)).astype(BF16)

    def decode(m, out_ref, slot, keep):
        features = (dot(counts_ref[...], upd_ref[m]) / K_DEC).astype(BF16)
        if keep:
            feat_ref[slot] = features
        x = grid_ref[...].astype(F32) + dot_nt(readout_ref[...], features)
        out_ref[slot] = x.astype(BF16)

    for m in range(own):
        decode(m, x_ref, m, True)
    for m in range(own, members):
        decode(m, extra_ref, m - own, False)


def pair_list(own, other):
    pairs = [(i, j) for i in range(own) for j in range(i + 1, own)]
    cross = [(i, own + j) for i in range(own) for j in range(other)]
    return pairs, cross


def stats_kernel(members, target_ref, *refs):
    out_ref = refs[-1]
    xs = [r[i].astype(F32) for r in refs[:-1] for i in range(r.shape[0])]
    truth = target_ref[...].astype(F32)
    pairs, cross = pair_list(members, len(xs) - members)
    rows = []

    def lane_sums(diff):
        col = jnp.sum(diff * diff, axis=0, keepdims=True)
        total = col[:, :LANES]
        for c in range(1, col.shape[1] // LANES):
            total = total + col[:, c * LANES : (c + 1) * LANES]
        return total

    for i in range(members):
        rows.append(lane_sums(xs[i] - truth))
    for i, j in pairs + cross:
        rows.append(lane_sums(xs[i] - xs[j]))
    row_id = lax.broadcasted_iota(jnp.int32, (32, LANES), 0)
    lane_id = lax.broadcasted_iota(jnp.int32, (32, LANES), 1)
    table = jnp.zeros((32, LANES), F32)
    for k, row in enumerate(rows):
        table = jnp.where(row_id == k, row, table)
    sums = jnp.sum(table, axis=1, keepdims=True)
    line = jnp.sum(jnp.where(row_id == lane_id, sums, 0.0), axis=0, keepdims=True)
    out_ref[...] = jnp.broadcast_to(line[None], out_ref.shape)


def slope_kernel(
    members, members_all, stat_ref, target_ref, *refs
):
    parts = (len(refs) - 3) // 3
    grad_ref, score_ref, pack_ref = refs[-3:]
    xs = [r[i] for r in refs[: 2 * parts] for i in range(r.shape[0])]
    feats = [r.at[i] for r in refs[2 * parts : 3 * parts] for i in range(r.shape[0])]
    xf = [x.astype(F32) for x in xs]
    truth = target_ref[...].astype(F32)
    pairs, cross = pair_list(members, members)
    total = jnp.sum(stat_ref[...].reshape(stat_ref.shape[0], LANES), axis=0, keepdims=True)
    dist = jnp.sqrt(total + EPSILON)
    lane = lax.broadcasted_iota(jnp.int32, (1, LANES), 1)
    first_cross = members + len(pairs)
    end = first_cross + len(cross)
    m = float(members_all)
    share = jnp.where(
        lane < members,
        1.0 / m,
        jnp.where(lane < first_cross, -1.0 / (m * m), jnp.where(lane < end, -0.5 / (m * m), 0.0)),
    )
    score = jnp.sum(dist * share, axis=1, keepdims=True)
    score_ref[...] = jnp.broadcast_to(score, score_ref.shape)
    pull = 1.0 / (jnp.where(lane < members, m, m * m) * dist)
    coef = {}
    for k, (i, j) in enumerate(pairs + cross):
        value = pull[:, members + k : members + k + 1]
        coef[i, j] = value
        coef[j, i] = value
    acc = None
    for i in range(members):
        slope = pull[:, i : i + 1] * (xf[i] - truth)
        for j in range(2 * members):
            if j != i:
                slope = slope + coef[i, j] * (xf[j] - xf[i])
        part = dot(slope.astype(BF16), feats[i][...])
        acc = part if acc is None else acc + part
    v, d = acc.shape
    pack_ref[...] = jnp.zeros_like(pack_ref)
    for c in range(d // LANES):
        pack_ref[c * v : (c + 1) * v, :] = acc[:, c * LANES : (c + 1) * LANES]
    grad_ref[...] = pack_ref[...].astype(BF16).reshape(grad_ref.shape)


def share_kernel(spare, recv_ref, score_ref, out_ref):
    total = jnp.sum(recv_ref[...].astype(F32), axis=0)
    rows = lax.broadcasted_iota(jnp.int32, total.shape, 0)
    last = lax.axis_index("space") == lax.axis_size("space") - 1
    score = jnp.broadcast_to(score_ref[0:1, :], total.shape)
    total = jnp.where(jnp.logical_and(last, rows >= spare), score, total)
    out_ref[...] = jnp.broadcast_to(total[None], out_ref.shape)


def spread_kernel(spare, recv_ref, out_ref):
    total = jnp.sum(recv_ref[...], axis=0)
    rows = lax.broadcasted_iota(jnp.int32, total.shape, 0)
    last = lax.axis_index("space") == lax.axis_size("space") - 1
    high = total.astype(BF16)
    low = (total - high.astype(F32)).astype(BF16)
    sent = jnp.where(jnp.logical_and(last, rows > spare), low.astype(F32), high.astype(F32)).astype(BF16)
    out_ref[...] = jnp.broadcast_to(sent[None], out_ref.shape)


def final_kernel(scale, recv_ref, out_ref, objective_ref, pack_ref):
    v, d = out_ref.shape
    used = v * d // LANES
    pack_ref[...] = recv_ref[...].reshape(pack_ref.shape).astype(F32)
    tail = pack_ref[used : used + 8, :]
    objective_ref[0] = jnp.max(tail[0:1, :] + tail[1:2, :]) * scale
    grad = pack_ref[:used, :]
    square = jnp.sum(jnp.sum(grad * grad, axis=0, keepdims=True), axis=1, keepdims=True)
    factor = 1.0 / jnp.sqrt(square / (v * d) + EPSILON)
    for c in range(d // LANES):
        out_ref[:, c * LANES : (c + 1) * LANES] = pack_ref[c * v : (c + 1) * v, :] * factor


def exchange(blocks, axis):
    return lax.all_to_all(blocks, axis, split_axis=0, concat_axis=0, tiled=True)


def step(
    grid_in,
    target,
    noise,
    neighbours,
    enc_index,
    dec_index,
    w_in,
    w_gamma,
    w_beta,
    w_qkv,
    w_o,
    readout_matrix,
):
    tok = enc_index.shape[0]
    points = dec_index.shape[0]
    d = w_o.shape[0]
    members = noise.shape[1]
    v = grid_in.shape[1]
    space = lax.axis_size("space")
    grid = grid_in[0]
    truth = target[0]

    pooled = call(
        pool_kernel,
        pltpu.VMEM((v + members, tok), F32),
        (enc_index.T, grid, noise[0]),
        hbm=(0, 1, 2),
        scratch=(
            pltpu.VMEM((enc_index.shape[1], tok), jnp.int32),
            pltpu.VMEM((v, points), BF16),
            pltpu.VMEM(noise.shape[1:], F32),
            pltpu.SemaphoreType.DMA((3,)),
        ),
        work=4 * 10**9,
    )
    pairs = [(q * space + i, (1 - q) * space + (i ^ 1)) for q in range(2) for i in range(space)]
    nexts = [(i, (i + 1 if i % 2 else i - 1) % space) for i in range(space)]
    from_pair = lax.ppermute(pooled, ("member", "space"), pairs)
    from_next = lax.ppermute(pooled, "space", nexts)
    states, gain, shift, project, counts = call(
        own_kernel,
        [
            pltpu.VMEM((tok, d), F32),
            pltpu.VMEM((members, d), F32),
            pltpu.VMEM((members, d), F32),
            pltpu.VMEM((members * tok, 3 * d), BF16),
            pltpu.VMEM((points, 2 * tok), BF16),
        ],
        (pooled, w_in, noise[0], w_gamma, w_beta, w_qkv, dec_index.T),
        scratch=(pltpu.VMEM((members * tok, d), BF16),),
        work=4 * 10**9,
    )
    half = members // 2
    forecasts = pltpu.VMEM((half, v, points), BF16)

    def run(begin, extra_out, halo, slots):
        scratch = [
            pltpu.VMEM((2 * slots * tok, d), BF16),
            pltpu.VMEM((slots, 3 * tok, 2 * d), BF16),
            pltpu.VMEM((slots * tok, d), BF16),
            pltpu.VMEM((slots, 2 * tok, d), BF16),
        ]
        if slots > half:
            scratch.append(pltpu.VMEM(((slots - half) * tok, 3 * d), BF16))
        return call(
            functools.partial(members_kernel, begin, half),
            [forecasts, pltpu.VMEM((half, points, d), BF16), extra_out],
            (
                neighbours,
                *halo,
                w_in,
                w_gamma,
                w_beta,
                gain,
                shift,
                project,
                states,
                counts,
                grid,
                w_qkv,
                w_o,
                readout_matrix,
            ),
            smem=(0,),
            scratch=scratch,
            limit=36,
            work=8 * 10**9,
        )

    x_a, feat_a, normed = run(0, pltpu.VMEM((2 * tok, d), F32), (from_pair, from_next), half)
    got_a = lax.ppermute(x_a, "member", [(0, 1), (1, 0)])
    x_b, feat_b, got_b = run(half, forecasts, (normed, from_pair), members)
    own, other, feats = [x_a, x_b], [got_a, got_b], [feat_a, feat_b]
    pred = jnp.concatenate(own, axis=0)
    members_all = members * lax.axis_size("member")
    stats = call(
        functools.partial(stats_kernel, members),
        pltpu.VMEM((space, 1, LANES), F32),
        (truth, *own, *other),
        work=10**9,
    )
    stats = exchange(stats, "space")
    rows = -(-v * d // (LANES * space * 8)) * 8
    grad, score = call(
        functools.partial(slope_kernel, members, members_all),
        [
            pltpu.VMEM((space, rows, LANES), BF16),
            pltpu.VMEM((8, LANES), F32),
        ],
        (stats, truth, *own, *other, *feats),
        scratch=(pltpu.VMEM((space * rows, LANES), F32),),
    )
    grad = exchange(grad, "space")
    peers = lax.axis_size("dp") * lax.axis_size("member")
    spare = v * d // LANES - (space - 1) * rows
    assert 0 < spare <= rows - 2
    share = call(
        functools.partial(share_kernel, spare), pltpu.VMEM((peers, rows, LANES), F32), (grad, score)
    )
    share = exchange(share, ("dp", "member"))
    scale = 1.0 / (lax.axis_size("dp") * (v * points * space) ** 0.5)
    spread = call(
        functools.partial(spread_kernel, spare), pltpu.VMEM((space, rows, LANES), BF16), (share,)
    )
    spread = exchange(spread, "space")
    unit, objective = call(
        functools.partial(final_kernel, scale),
        [jax.ShapeDtypeStruct((v, d), F32), jax.ShapeDtypeStruct((1,), F32)],
        (spread,),
        out_specs=[VMEM, SMEM],
        scratch=(pltpu.VMEM((space * rows, LANES), F32),),
    )
    return (pred[None], objective.reshape(()), unit)


def solution(mesh):
    in_specs = (
        P("dp", None, "space"),
        P("dp", None, "space"),
        P("dp", "member", None),
        P("space", None),
        P("space", None),
        P("space", None),
        P(),
        P(),
        P(),
        P(),
        P(),
        P(),
    )
    out_specs = (P("dp", "member", None, "space"), P(), P())
    return jax.shard_map(step, mesh=mesh, in_specs=in_specs, out_specs=out_specs, check_vma=False)
```

```python
import functools

import jax
import jax.numpy as jnp
from jax import lax
from jax.experimental import pallas as pl
from jax.experimental.pallas import tpu as pltpu
from jax.sharding import PartitionSpec as P

HEADS = 12
HD = 64
WIN = 64
K_ENC = 4
K_DEC = 3
EPSILON = 1e-06
LANES = 128
GROUP = (4, 2)
PART = (2, 2)

F32 = jnp.float32
BF16 = jnp.bfloat16

VMEM = pl.BlockSpec(memory_space=pltpu.VMEM)
SMEM = pl.BlockSpec(memory_space=pltpu.SMEM)
HBM = pl.BlockSpec(memory_space=pltpu.HBM)
NT = (((1,), (1,)), ((), ()))


def dot(a, b):
    return jnp.dot(a, b, preferred_element_type=F32)


def dot_nt(a, b):
    return lax.dot_general(a, b, NT, preferred_element_type=F32)


def call(kernel, outs, args, smem=(), hbm=(), scratch=(), out_specs=None, limit=24, work=0):
    many = isinstance(outs, list)
    kept = [
        a if i in smem else pltpu.with_memory_space_constraint(a, pltpu.HBM if i in hbm else pltpu.VMEM)
        for i, a in enumerate(args)
    ]
    return pl.pallas_call(
        kernel,
        out_shape=outs,
        in_specs=[SMEM if i in smem else HBM if i in hbm else VMEM for i in range(len(args))],
        out_specs=out_specs or ([VMEM] * len(outs) if many else VMEM),
        scratch_shapes=list(scratch),
        compiler_params=pltpu.CompilerParams(vmem_limit_bytes=limit << 20),
        cost_estimate=pl.CostEstimate(flops=work, transcendentals=0, bytes_accessed=work // 100),
    )(*kept)


def counts_of(index_rows, targets):
    many = index_rows.shape[1]
    local = lax.rem(index_rows, jnp.int32(targets))
    positions = lax.broadcasted_iota(jnp.int32, (targets, many), 0)
    counts = (local[0:1, :] == positions).astype(F32)
    for row in range(1, index_rows.shape[0]):
        counts = counts + (local[row : row + 1, :] == positions).astype(F32)
    return counts


def pool_kernel(enc_hbm, grid_hbm, noise_hbm, pooled_ref, enc_ref, grid_ref, noise_ref, sems):
    copies = [
        pltpu.make_async_copy(enc_hbm, enc_ref, sems.at[0]),
        pltpu.make_async_copy(grid_hbm, grid_ref, sems.at[1]),
        pltpu.make_async_copy(noise_hbm, noise_ref, sems.at[2]),
    ]
    for copy in copies:
        copy.start()
    copies[0].wait()
    counts = counts_of(enc_ref[...], grid_ref.shape[1]).astype(BF16)
    copies[1].wait()
    copies[2].wait()
    v = grid_ref.shape[0]
    pooled_ref[:v, :] = dot(grid_ref[...], counts) * (1.0 / K_ENC)
    pooled_ref[v:, :] = jnp.zeros((pooled_ref.shape[0] - v, pooled_ref.shape[1]), F32)
    members, nz = noise_ref.shape
    pooled_ref[v : v + members, :nz] = noise_ref[...]


def states_of(pooled, w_in):
    values = pooled[: w_in.shape[0]].T
    high = values.astype(BF16)
    rest = values - high.astype(F32)
    mid = rest.astype(BF16)
    low = (rest - mid.astype(F32)).astype(BF16)
    return dot(high, w_in) + (dot(mid, w_in) + dot(low, w_in))


def normed_of(states):
    centre = states - jnp.mean(states, axis=-1, keepdims=True)
    spread = jnp.mean(centre * centre, axis=-1, keepdims=True)
    return centre / jnp.sqrt(spread + EPSILON)


def conditioning(noise, w_gamma, w_beta):
    gain = 1.0 + jnp.dot(noise, w_gamma, precision=lax.Precision.HIGHEST)
    return gain, jnp.dot(noise, w_beta, precision=lax.Precision.HIGHEST)


def project_into(out_ref, inputs, w_qkv_ref):
    d = w_qkv_ref.shape[0]
    for c in range(3):
        part = dot(inputs, w_qkv_ref[:, c * d : (c + 1) * d])
        if c == 0:
            part = part * HD ** (-0.5)
        out_ref[:, c * d : (c + 1) * d] = part.astype(BF16)


def own_kernel(
    pooled_ref,
    w_in_ref,
    noise_ref,
    w_gamma_ref,
    w_beta_ref,
    w_qkv_ref,
    dec_ref,
    states_ref,
    gain_ref,
    shift_ref,
    project_ref,
    counts_ref,
    inputs_ref,
):
    tok, _ = states_ref.shape
    members = noise_ref.shape[0]
    gain, shift = conditioning(noise_ref[...], w_gamma_ref[...], w_beta_ref[...])
    gain_ref[...] = gain
    shift_ref[...] = shift
    states = states_of(pooled_ref[...], w_in_ref[...])
    states_ref[...] = states
    normed = normed_of(states)
    for m in range(members):
        inputs_ref[m * tok : (m + 1) * tok, :] = (normed * gain[m : m + 1] + shift[m : m + 1]).astype(BF16)
    project_into(project_ref, inputs_ref[...], w_qkv_ref)
    counts = counts_of(dec_ref[...], tok).T.astype(BF16)
    counts_ref[:, :tok] = counts
    counts_ref[:, tok:] = counts


def members_kernel(
    begin,
    own,
    nbr_ref,
    pair_ref,
    next_ref,
    w_in_ref,
    w_gamma_ref,
    w_beta_ref,
    gain_ref,
    shift_ref,
    project_ref,
    states_ref,
    counts_ref,
    grid_ref,
    w_qkv_ref,
    w_o_ref,
    readout_ref,
    x_ref,
    feat_ref,
    extra_ref,
    *refs,
):
    tok, d = states_ref.shape
    parted = [refs[4 * i : 4 * i + 4] for i in range(len(refs) // 4)]
    each = parted[0][1].shape[0]
    members = each * len(parted)
    wins = tok // WIN
    group = GROUP[begin > 0]
    wide = group * HD
    windows = wins * lax.axis_size("space")
    first = lax.axis_index("space") * wins
    gains = [gain_ref[begin + m : begin + m + 1, :] for m in range(own)]
    shifts = [shift_ref[begin + m : begin + m + 1, :] for m in range(own)]
    sources = [(project_ref, (begin + m) * tok) for m in range(own)]
    if members > own:
        mine_ref = refs[-1]
        v, count = w_in_ref.shape[0], gain_ref.shape[0]
        noise = next_ref[v : v + count, : w_gamma_ref.shape[0]]
        gain, shift = conditioning(noise, w_gamma_ref[...], w_beta_ref[...])
        for m in range(members - own):
            k = begin + m
            gains.append(gain[k : k + 1])
            shifts.append(shift[k : k + 1])
            sources.append((mine_ref, m * tok))
    odd = lax.rem(lax.axis_index("space"), 2) == 1
    sides = []
    for slot in range(2):
        if begin == 0:
            pooled = jnp.where(odd == (slot == 0), pair_ref[...], next_ref[...])
            sides.append(normed_of(states_of(pooled, w_in_ref[...])))
            extra_ref[slot * tok : (slot + 1) * tok, :] = sides[-1]
        else:
            sides.append(pair_ref[slot * tok : (slot + 1) * tok, :])
    head_of = lax.broadcasted_iota(jnp.int32, (WIN, wide), 1) // HD
    starts = []
    for w in range(wins):
        starts.append([(wins + w) * WIN])
        for j in range(nbr_ref.shape[1]):
            reach = lax.rem(nbr_ref[w, j] - first - w + 2 + windows, windows) + w
            starts[w].append(pl.multiple_of(reach * WIN, WIN))

    def project(p):
        edge_ref, kv_ref, _, _ = parted[p]
        if p * each >= own:
            normed = normed_of(states_ref[...])
            ms = range(p * each, (p + 1) * each)
            rows = [(normed * gains[m] + shifts[m]).astype(BF16) for m in ms]
            lo = (p * each - own) * tok
            project_into(mine_ref.at[lo : lo + each * tok], jnp.concatenate(rows, axis=0), w_qkv_ref)
        for m in range(each):
            k = p * each + m
            for slot in range(2):
                row = (2 * m + slot) * tok
                edge_ref[row : row + tok, :] = (sides[slot] * gains[k] + shifts[k]).astype(BF16)
        for c in range(2):
            lo = c * d
            part = dot(edge_ref[...], w_qkv_ref[:, d + lo : d + lo + d]).astype(BF16)
            for m in range(each):
                kv_ref[m, :tok, lo : lo + d] = part[2 * m * tok : (2 * m + 1) * tok]
                ref, row = sources[p * each + m]
                kv_ref[m, tok : 2 * tok, lo : lo + d] = ref[row : row + tok, d + lo : d + lo + d]
                kv_ref[m, 2 * tok :, lo : lo + d] = part[(2 * m + 1) * tok : (2 * m + 2) * tok]

    def attend(p):
        _, kv_ref, att_ref, _ = parted[p]
        for m in range(each):
            ref, base = sources[p * each + m]
            for w in range(wins):
                row = m * tok + w * WIN
                for g in range(HEADS // group):
                    lo = g * wide
                    q = ref[base + w * WIN : base + (w + 1) * WIN, lo : lo + wide]
                    zero = jnp.zeros_like(q)
                    spread = jnp.concatenate(
                        [jnp.where(head_of == h, q, zero) for h in range(group)], axis=0
                    )
                    keys = jnp.concatenate(
                        [kv_ref[m, pl.ds(s, WIN), lo : lo + wide] for s in starts[w]], axis=0
                    )
                    values = jnp.concatenate(
                        [kv_ref[m, pl.ds(s, WIN), d + lo : d + lo + wide] for s in starts[w]], axis=0
                    )
                    scores = dot_nt(spread, keys)
                    top = jnp.max(scores, axis=-1, keepdims=True)
                    weights = jnp.exp(scores - top)
                    weights = weights * (1.0 / jnp.sum(weights, axis=-1, keepdims=True))
                    mixed = dot(weights.astype(BF16), values)
                    out = mixed[:WIN]
                    for h in range(1, group):
                        out = jnp.where(head_of == h, mixed[h * WIN : (h + 1) * WIN], out)
                    att_ref[row : row + WIN, lo : lo + wide] = out.astype(BF16)

    def decode(p):
        _, _, att_ref, upd_ref = parted[p]
        mixed = dot(att_ref[...], w_o_ref[...])
        for m in range(each):
            updated = (states_ref[...] + mixed[m * tok : (m + 1) * tok]) * (1.0 / K_DEC)
            high = updated.astype(BF16)
            upd_ref[m, :tok, :] = high
            upd_ref[m, tok:, :] = (updated - high.astype(F32)).astype(BF16)
        for m in range(each):
            k = p * each + m
            features = dot(counts_ref[...], upd_ref[m]).astype(BF16)
            x = grid_ref[...].astype(F32) + dot_nt(readout_ref[...], features)
            if k < own:
                feat_ref[k] = features
                x_ref[k] = x.astype(BF16)
            else:
                extra_ref[k - own] = x.astype(BF16)

    project(0)
    for p in range(len(parted)):
        attend(p)
        if p + 1 < len(parted):
            project(p + 1)
        decode(p)


def pair_list(own, other):
    pairs = [(i, j) for i in range(own) for j in range(i + 1, own)]
    cross = [(i, own + j) for i in range(own) for j in range(other)]
    return pairs, cross


def stats_kernel(members, target_ref, *refs):
    out_ref = refs[-1]
    xs = [r[i].astype(F32) for r in refs[:-1] for i in range(r.shape[0])]
    truth = target_ref[...].astype(F32)
    pairs, cross = pair_list(members, len(xs) - members)
    rows = []

    def lane_sums(diff):
        col = jnp.sum(diff * diff, axis=0, keepdims=True)
        total = col[:, :LANES]
        for c in range(1, col.shape[1] // LANES):
            total = total + col[:, c * LANES : (c + 1) * LANES]
        return total

    for i in range(members):
        rows.append(lane_sums(xs[i] - truth))
    for i, j in pairs + cross:
        rows.append(lane_sums(xs[i] - xs[j]))
    row_id = lax.broadcasted_iota(jnp.int32, (32, LANES), 0)
    lane_id = lax.broadcasted_iota(jnp.int32, (32, LANES), 1)
    table = jnp.zeros((32, LANES), F32)
    for k, row in enumerate(rows):
        table = jnp.where(row_id == k, row, table)
    sums = jnp.sum(table, axis=1, keepdims=True)
    line = jnp.sum(jnp.where(row_id == lane_id, sums, 0.0), axis=0, keepdims=True)
    out_ref[...] = jnp.broadcast_to(line[None], out_ref.shape)


def slope_kernel(
    members, members_all, stat_ref, target_ref, *refs
):
    parts = (len(refs) - 3) // 3
    grad_ref, score_ref, pack_ref = refs[-3:]
    xs = [r[i] for r in refs[: 2 * parts] for i in range(r.shape[0])]
    feats = [r.at[i] for r in refs[2 * parts : 3 * parts] for i in range(r.shape[0])]
    xf = [x.astype(F32) for x in xs]
    truth = target_ref[...].astype(F32)
    pairs, cross = pair_list(members, members)
    total = jnp.sum(stat_ref[...].reshape(stat_ref.shape[0], LANES), axis=0, keepdims=True)
    dist = jnp.sqrt(total + EPSILON)
    lane = lax.broadcasted_iota(jnp.int32, (1, LANES), 1)
    first_cross = members + len(pairs)
    end = first_cross + len(cross)
    m = float(members_all)
    share = jnp.where(
        lane < members,
        1.0 / m,
        jnp.where(lane < first_cross, -1.0 / (m * m), jnp.where(lane < end, -0.5 / (m * m), 0.0)),
    )
    score = jnp.sum(dist * share, axis=1, keepdims=True)
    score_ref[...] = jnp.broadcast_to(score, score_ref.shape)
    pull = 1.0 / (jnp.where(lane < members, m, m * m) * dist)
    coef = {}
    for k, (i, j) in enumerate(pairs + cross):
        value = pull[:, members + k : members + k + 1]
        coef[i, j] = value
        coef[j, i] = value
    acc = None
    for i in range(members):
        slope = pull[:, i : i + 1] * (xf[i] - truth)
        for j in range(2 * members):
            if j != i:
                slope = slope + coef[i, j] * (xf[j] - xf[i])
        part = dot(slope.astype(BF16), feats[i][...])
        acc = part if acc is None else acc + part
    v, d = acc.shape
    pack_ref[...] = jnp.zeros_like(pack_ref)
    for c in range(d // LANES):
        pack_ref[c * v : (c + 1) * v, :] = acc[:, c * LANES : (c + 1) * LANES]
    grad_ref[...] = pack_ref[...].astype(BF16).reshape(grad_ref.shape)


def share_kernel(spare, recv_ref, score_ref, out_ref):
    total = jnp.sum(recv_ref[...].astype(F32), axis=0)
    rows = lax.broadcasted_iota(jnp.int32, total.shape, 0)
    last = lax.axis_index("space") == lax.axis_size("space") - 1
    score = jnp.broadcast_to(score_ref[0:1, :], total.shape)
    total = jnp.where(jnp.logical_and(last, rows >= spare), score, total)
    out_ref[...] = jnp.broadcast_to(total[None], out_ref.shape)


def spread_kernel(spare, recv_ref, out_ref):
    total = jnp.sum(recv_ref[...], axis=0)
    rows = lax.broadcasted_iota(jnp.int32, total.shape, 0)
    last = lax.axis_index("space") == lax.axis_size("space") - 1
    high = total.astype(BF16)
    low = (total - high.astype(F32)).astype(BF16)
    sent = jnp.where(jnp.logical_and(last, rows > spare), low.astype(F32), high.astype(F32)).astype(BF16)
    out_ref[...] = jnp.broadcast_to(sent[None], out_ref.shape)


def final_kernel(scale, recv_ref, out_ref, objective_ref, pack_ref):
    v, d = out_ref.shape
    used = v * d // LANES
    pack_ref[...] = recv_ref[...].reshape(pack_ref.shape).astype(F32)
    tail = pack_ref[used : used + 8, :]
    objective_ref[0] = jnp.max(tail[0:1, :] + tail[1:2, :]) * scale
    grad = pack_ref[:used, :]
    square = jnp.sum(jnp.sum(grad * grad, axis=0, keepdims=True), axis=1, keepdims=True)
    factor = 1.0 / jnp.sqrt(square / (v * d) + EPSILON)
    for c in range(d // LANES):
        out_ref[:, c * LANES : (c + 1) * LANES] = pack_ref[c * v : (c + 1) * v, :] * factor


def exchange(blocks, axis):
    return lax.all_to_all(blocks, axis, split_axis=0, concat_axis=0, tiled=True)


def step(
    grid_in,
    target,
    noise,
    neighbours,
    enc_index,
    dec_index,
    w_in,
    w_gamma,
    w_beta,
    w_qkv,
    w_o,
    readout_matrix,
):
    tok = enc_index.shape[0]
    points = dec_index.shape[0]
    d = w_o.shape[0]
    members = noise.shape[1]
    v = grid_in.shape[1]
    space = lax.axis_size("space")
    grid = grid_in[0]
    truth = target[0]

    pooled = call(
        pool_kernel,
        pltpu.VMEM((v + members, tok), F32),
        (enc_index.T, grid, noise[0]),
        hbm=(0, 1, 2),
        scratch=(
            pltpu.VMEM((enc_index.shape[1], tok), jnp.int32),
            pltpu.VMEM((v, points), BF16),
            pltpu.VMEM(noise.shape[1:], F32),
            pltpu.SemaphoreType.DMA((3,)),
        ),
        work=4 * 10**9,
    )
    pairs = [(q * space + i, (1 - q) * space + (i ^ 1)) for q in range(2) for i in range(space)]
    nexts = [(i, (i + 1 if i % 2 else i - 1) % space) for i in range(space)]
    from_pair = lax.ppermute(pooled, ("member", "space"), pairs)
    from_next = lax.ppermute(pooled, "space", nexts)
    states, gain, shift, project, counts = call(
        own_kernel,
        [
            pltpu.VMEM((tok, d), F32),
            pltpu.VMEM((members, d), F32),
            pltpu.VMEM((members, d), F32),
            pltpu.VMEM((members * tok, 3 * d), BF16),
            pltpu.VMEM((points, 2 * tok), BF16),
        ],
        (pooled, w_in, noise[0], w_gamma, w_beta, w_qkv, dec_index.T),
        scratch=(pltpu.VMEM((members * tok, d), BF16),),
        work=4 * 10**9,
    )
    half = members // 2
    forecasts = pltpu.VMEM((half, v, points), BF16)

    def run(begin, extra_out, halo, slots):
        each = PART[begin > 0]
        scratch = [
            pltpu.VMEM((2 * each * tok, d), BF16),
            pltpu.VMEM((each, 3 * tok, 2 * d), BF16),
            pltpu.VMEM((each * tok, d), BF16),
            pltpu.VMEM((each, 2 * tok, d), BF16),
        ] * (slots // each)
        if slots > half:
            scratch.append(pltpu.VMEM(((slots - half) * tok, 3 * d), BF16))
        return call(
            functools.partial(members_kernel, begin, half),
            [forecasts, pltpu.VMEM((half, points, d), BF16), extra_out],
            (
                neighbours,
                *halo,
                w_in,
                w_gamma,
                w_beta,
                gain,
                shift,
                project,
                states,
                counts,
                grid,
                w_qkv,
                w_o,
                readout_matrix,
            ),
            smem=(0,),
            scratch=scratch,
            limit=36,
            work=8 * 10**9,
        )

    x_a, feat_a, normed = run(0, pltpu.VMEM((2 * tok, d), F32), (from_pair, from_next), half)
    got_a = lax.ppermute(x_a, "member", [(0, 1), (1, 0)])
    x_b, feat_b, got_b = run(half, forecasts, (normed, from_pair), members)
    own, other, feats = [x_a, x_b], [got_a, got_b], [feat_a, feat_b]
    pred = jnp.concatenate(own, axis=0)
    members_all = members * lax.axis_size("member")
    stats = call(
        functools.partial(stats_kernel, members),
        pltpu.VMEM((space, 1, LANES), F32),
        (truth, *own, *other),
        work=10**9,
    )
    stats = exchange(stats, "space")
    rows = -(-v * d // (LANES * space * 8)) * 8
    grad, score = call(
        functools.partial(slope_kernel, members, members_all),
        [
            pltpu.VMEM((space, rows, LANES), BF16),
            pltpu.VMEM((8, LANES), F32),
        ],
        (stats, truth, *own, *other, *feats),
        scratch=(pltpu.VMEM((space * rows, LANES), F32),),
    )
    grad = exchange(grad, "space")
    peers = lax.axis_size("dp") * lax.axis_size("member")
    spare = v * d // LANES - (space - 1) * rows
    assert 0 < spare <= rows - 2
    share = call(
        functools.partial(share_kernel, spare), pltpu.VMEM((peers, rows, LANES), F32), (grad, score)
    )
    share = exchange(share, ("dp", "member"))
    scale = 1.0 / (lax.axis_size("dp") * (v * points * space) ** 0.5)
    spread = call(
        functools.partial(spread_kernel, spare), pltpu.VMEM((space, rows, LANES), BF16), (share,)
    )
    spread = exchange(spread, "space")
    unit, objective = call(
        functools.partial(final_kernel, scale),
        [jax.ShapeDtypeStruct((v, d), F32), jax.ShapeDtypeStruct((1,), F32)],
        (spread,),
        out_specs=[VMEM, SMEM],
        scratch=(pltpu.VMEM((space * rows, LANES), F32),),
    )
    return (pred[None], objective.reshape(()), unit)


def solution(mesh):
    in_specs = (
        P("dp", None, "space"),
        P("dp", None, "space"),
        P("dp", "member", None),
        P("space", None),
        P("space", None),
        P("space", None),
        P(),
        P(),
        P(),
        P(),
        P(),
        P(),
    )
    out_specs = (P("dp", "member", None, "space"), P(), P())
    return jax.shard_map(step, mesh=mesh, in_specs=in_specs, out_specs=out_specs, check_vma=False)
```
